256 devices in a mesh: tile: 32 (over x, z), slide: 8 (over y, core).
Axes of the slice: x: 4, y: 4, z: 8, core: 2. Of those that a mesh axis runs over, the one named last changes fastest.
Arguments:
- tiles: bfloat16 [8, 96, 7, 7, 2048], P('slide', 'tile'), may hold values from -6 to 6
- tile_counts: int32 [8, 32], P('slide', 'tile'), may hold values from 1 to 3, as said below
- tile_weights: float32 [8, 96], P('slide', 'tile'), may hold values from 0.1 to 2
- slide_of: int32 [8, 96, 1], P('slide', 'tile'), may hold values from 0 to 31, as said below
- owner_map: int32 [8, 32], P('slide'), may hold values from 0 to 31, each once within a row
- cotangent: bfloat16 [8, 32, 2048], P('slide', 'tile'), may hold values from -6 to 6
- conv_weight: bfloat16 [9, 64, 2048], replicated, may hold values from -0.25 to 0.25
Outputs:
- pooled: float32 [8, 32, 2048], P('slide', 'tile')
- input_grads: float32 [8, 96, 7, 7, 2048], P('slide', 'tile')
- weight_grads: float32 [9, 64, 2048], P(None, None, 'tile')
The draws below stay inside these ranges and needn't reach their ends.
Inputs may be any that keep to these rules, and one draw needn't show every extreme that they name: On every device the live tiles are the first tile_counts slots; in each slide group one device has all 3 slots live. `slide_of`: in each slide group, max(1, 8) slides name exactly one slot each, the first slot of some device; the other slots name the remaining slides evenly at random.
All inputs are finite; a program needn't handle non-finite values.
Results may differ from the reference program's by a relative error of at most 0.0065.
Values may be sent and summed in bfloat16 or wider, within the bound.
A program may use at most 128 MiB of HBM per device.

```python
import math
import jax
import jax.numpy as jnp
from jax import lax

CHANNELS = 2048
GROUPS = 32
SIDE = 7
SLOTS = 3
GROUP_WIDTH = 64
TILES_GROUP = 96
N_TILE = 32
N_SLIDE = 8


def draw_tiles(key, part):
    key_noise, key_mean = jax.random.split(key, 2)
    full_shape = (N_SLIDE, TILES_GROUP, SIDE, SIDE, CHANNELS)
    mean_shape = (N_SLIDE, TILES_GROUP, 1, 1, CHANNELS)
    noise_part = jax.random.normal(key_noise, full_shape, jnp.float32) * 0.7
    tile_mean = jax.random.normal(key_mean, mean_shape, jnp.float32) * 0.8
    values = noise_part + tile_mean
    return jnp.clip(values, -6.0, 6.0).astype(jnp.bfloat16)


def draw_tile_counts(key, part):
    key_count, key_pick = jax.random.split(key)
    drawn = jax.random.randint(key_count, (N_SLIDE, N_TILE), 1, SLOTS + 1)
    picked = jax.random.randint(key_pick, (N_SLIDE, 1), 0, N_TILE)
    column = jnp.arange(N_TILE, dtype=jnp.int32)[None, :]
    return jnp.where(column == picked, SLOTS, drawn).astype(jnp.int32)


def shuffle_devices(subkey):
    return jax.random.permutation(subkey, N_TILE).astype(jnp.int32)


def draw_slide_of(key, part):
    key_dense, key_chosen, key_label = jax.random.split(jax.random.fold_in(key, 17), 3)
    sparse_count = max(1, N_TILE // 4)
    dense_count = N_TILE - sparse_count
    labels = jax.random.randint(key_dense, (N_SLIDE, TILES_GROUP), 0, dense_count).astype(jnp.int32)
    chosen = jax.vmap(shuffle_devices)(jax.random.split(key_chosen, N_SLIDE))
    positions = chosen[:, :sparse_count] * SLOTS
    group_rows = jnp.arange(N_SLIDE, dtype=jnp.int32)[:, None]
    sparse_labels = dense_count + jnp.arange(sparse_count, dtype=jnp.int32)[None, :]
    labels = labels.at[group_rows, positions].set(jnp.broadcast_to(sparse_labels, positions.shape))
    relabel = jax.vmap(shuffle_devices)(jax.random.split(key_label, N_SLIDE))
    return jnp.take_along_axis(relabel, labels, axis=1)[:, :, None].astype(jnp.int32)


def block_levels(own_key, dims, cuts, low, high):
    def one(axis_at, parts):
        steps = jax.random.uniform(jax.random.fold_in(jax.random.fold_in(own_key, 6), axis_at), (parts,), jnp.float32, low / len(cuts), high / len(cuts))
        return jnp.repeat(jnp.exp(steps), dims[axis_at] // parts).reshape((-1,) + (1,) * (len(dims) - axis_at - 1))

    factor_of = one(*cuts[0])
    for cut in cuts[1:]:
        factor_of = factor_of * one(*cut)
    return factor_of


def bell_draw(stream_key, dims, spread, most, cuts=(), kind=jnp.bfloat16):
    values = jax.random.normal(stream_key, dims, jnp.float32) * spread
    if len(cuts) > 0:
        values = block_levels(stream_key, dims, cuts, -0.22, 0.18) * values
    return jnp.clip(values, min=-most, max=most).astype(kind)


def setup_inputs(seed: int = 0) -> dict:
    streams_of = jax.random.split(jax.random.key(seed), 8)
    tiles = draw_tiles(jax.random.fold_in(streams_of[7], 71), 0)
    tile_counts = draw_tile_counts(jax.random.fold_in(streams_of[7], 71), 0)
    tile_weights = jnp.clip(jnp.exp(math.log(2.0) - 2.9957323 * jax.random.uniform(streams_of[2], (N_SLIDE, TILES_GROUP), jnp.float32) ** block_levels(streams_of[2], (N_SLIDE, TILES_GROUP), ((0, 8), (1, 32)), -0.2, 0.2)), 0.1, 2.0)
    slide_of = draw_slide_of(jax.random.fold_in(streams_of[7], 71), 0)
    owner_map = jax.vmap(lambda own: jax.random.permutation(own, N_TILE))(jax.random.split(streams_of[4], N_SLIDE)).reshape((N_SLIDE, N_TILE)).astype(jnp.int32)
    cotangent = bell_draw(streams_of[5], (N_SLIDE, N_TILE, CHANNELS), 1.0, 6.0, ((0, 8), (1, 32)))
    conv_weight = bell_draw(streams_of[6], (9, GROUP_WIDTH, CHANNELS), (9 * GROUP_WIDTH) ** -0.5, 0.25)
    return {"tiles": tiles, "tile_counts": tile_counts, "tile_weights": tile_weights, "slide_of": slide_of, "owner_map": owner_map, "cotangent": cotangent, "conv_weight": conv_weight}


loss_scale = 512.0


def conv_forward(features, weight):
    count_rows = features.shape[0]
    padded = jnp.pad(features.astype(jnp.float32), ((0, 0), (1, 1), (1, 1), (0, 0)))
    weight_f = weight.astype(jnp.float32)
    summed = jnp.zeros((count_rows, SIDE, SIDE, GROUPS, GROUP_WIDTH), jnp.float32)
    for offset in range(9):
        row_off, col_off = divmod(offset, 3)
        window = padded[:, row_off:row_off + SIDE, col_off:col_off + SIDE, :].reshape(count_rows, SIDE, SIDE, GROUPS, GROUP_WIDTH)
        tap = weight_f[offset].reshape(GROUP_WIDTH, GROUPS, GROUP_WIDTH)
        summed = summed + jnp.einsum("nhwgi,igo->nhwgo", window, tap)
    return summed.reshape(count_rows, SIDE, SIDE, CHANNELS)


def conv_backward(features, weight, pre_grad):
    count_rows = features.shape[0]
    padded = jnp.pad(features.astype(jnp.float32), ((0, 0), (1, 1), (1, 1), (0, 0)))
    weight_f = weight.astype(jnp.float32)
    grads_split = pre_grad.astype(jnp.float32).reshape(count_rows, SIDE, SIDE, GROUPS, GROUP_WIDTH)
    grads_padded = jnp.pad(grads_split, ((0, 0), (1, 1), (1, 1), (0, 0), (0, 0)))
    summed = jnp.zeros((count_rows, SIDE, SIDE, GROUPS, GROUP_WIDTH), jnp.float32)
    pieces = []
    for offset in range(9):
        row_off, col_off = divmod(offset, 3)
        window = padded[:, row_off:row_off + SIDE, col_off:col_off + SIDE, :].reshape(count_rows, SIDE, SIDE, GROUPS, GROUP_WIDTH)
        tap = weight_f[offset].reshape(GROUP_WIDTH, GROUPS, GROUP_WIDTH)
        pieces.append(jnp.einsum("nhwgi,nhwgo->igo", window, grads_split).reshape(GROUP_WIDTH, CHANNELS))
        shifted = grads_padded[:, 2 - row_off:2 - row_off + SIDE, 2 - col_off:2 - col_off + SIDE]
        summed = summed + jnp.einsum("nhwgo,igo->nhwgi", shifted, tap)
    input_grads = summed.reshape(count_rows, SIDE, SIDE, CHANNELS)
    return input_grads, jnp.stack(pieces, axis=0)


def reference(tiles, tile_counts, tile_weights, slide_of, owner_map, cotangent, conv_weight):
    slot_index = jnp.arange(TILES_GROUP, dtype=jnp.int32) % SLOTS
    device_of = jnp.arange(TILES_GROUP, dtype=jnp.int32) // SLOTS
    alive = (slot_index[None, :] < tile_counts[:, device_of]).astype(jnp.float32)
    tile_coef = alive * tile_weights
    target = jnp.take_along_axis(owner_map, slide_of[:, :, 0], axis=1)

    def one_group(packed):
        features, coef_row, target_row, cot_row = packed
        pre = conv_forward(features, conv_weight)
        embedding = jnp.mean(jax.nn.silu(pre), axis=(1, 2)).astype(jnp.bfloat16)
        owner_ids = jnp.arange(N_TILE, dtype=jnp.int32)
        routing = (target_row[None, :] == owner_ids[:, None]).astype(jnp.float32) * coef_row[None, :]
        numerator = jnp.dot(routing, embedding.astype(jnp.float32), precision=lax.Precision.HIGHEST)
        denominator = jnp.maximum(jnp.sum(routing, axis=1), 1.0)
        pooled = numerator / denominator[:, None]
        scaled = (loss_scale * cot_row.astype(jnp.float32) / denominator[:, None]).astype(jnp.bfloat16)
        tile_grads = jnp.dot(routing.T, scaled.astype(jnp.float32), precision=lax.Precision.HIGHEST)
        sigma = jax.nn.sigmoid(pre)
        slope = sigma * (1.0 + pre * (1.0 - sigma))
        pre_grad = (tile_grads[:, None, None, :] / (SIDE * SIDE) * slope).astype(jnp.bfloat16)
        input_grads, weight_terms = conv_backward(features, conv_weight, pre_grad)
        return pooled, input_grads, weight_terms

    pooled, input_grads, weight_terms = lax.map(one_group, (tiles, tile_coef, target, cotangent))
    weight_grads = jnp.sum(weight_terms, axis=0) / loss_scale
    return pooled, input_grads, weight_grads
```

```python
import functools

import jax
import jax.numpy as jnp
from jax import lax
from jax.experimental import pallas as pl
from jax.experimental.pallas import tpu as pltpu
from jax.sharding import PartitionSpec as P

MESH = pl.DeviceIdType.MESH
LOSS_SCALE = 512.0
SIDE = 7
SLOTS = 3
WIDTH = 64
LANES = 128
TAPS = 9
ROWS = SLOTS * 64
BASE = 16
PADDED = BASE + ROWS + 16
PACKED = TAPS * WIDTH // 2
f32 = jnp.float32
bf16 = jnp.bfloat16


class Sizes:
    def __init__(self, mesh):
        self.tiles = mesh.shape["tile"]
        self.slides = mesh.shape["slide"]
        self.ny = self.slides // 2
        self.nx = self.ny
        self.nz = self.tiles // self.nx
        self.pairs = self.tiles // 2
        self.piece = PACKED // self.nz


def position(sz):
    tile = lax.axis_index("tile")
    slide = lax.axis_index("slide")
    return tile, slide, tile // sz.nz, tile % sz.nz, slide // 2, slide % 2


def remote(src, dst, send, recv, device):
    return pltpu.make_async_remote_copy(
        src_ref=src, dst_ref=dst, send_sem=send, recv_sem=recv, device_id=device, device_id_type=MESH
    )


def signal(device):
    pl.semaphore_signal(pltpu.get_barrier_semaphore(), inc=1, device_id=device, device_id_type=MESH)


def slot_route(slot, counts, weights, slide_of, owner_map):
    coef = jnp.where(slot < counts[0, 0], weights[0, slot], 0.0)
    return coef, owner_map[0, slide_of[0, slot, 0]]


def gather_kernel(
    sz, counts, weights, slide_of, owner_map, cot, grad_out, den_out,
    stage, all_cot, my_total, z_total, x_total, total, zs, zr, xs, xr, tzs, tzr, txs, txr,
):
    tile, slide, x, z, y, c = position(sz)
    z_peers = [(x * sz.nz + (z + off) % sz.nz, slide) for off in range(1, sz.nz)]
    x_peers = [(((x + off) % sz.nx) * sz.nz + z, slide) for off in range(1, sz.nx)]
    for peer in z_peers + x_peers:
        signal(peer)
    for j in range(sz.pairs):
        stage[pl.ds(j, 1), :] = cot[0, :, pl.ds(j * LANES, LANES)].astype(f32)
    all_cot[tile] = stage[...].astype(bf16)
    lane = lax.broadcasted_iota(jnp.int32, (8, LANES), 1)
    routes = [slot_route(s, counts, weights, slide_of, owner_map) for s in range(SLOTS)]
    mine = jnp.zeros((8, LANES), f32)
    for coef, target in routes:
        mine = mine + jnp.where(lane == target, coef, 0.0)
    my_total[...] = mine
    pl.semaphore_wait(pltpu.get_barrier_semaphore(), len(z_peers) + len(x_peers))

    copies = []
    for i, peer in enumerate(z_peers):
        copies.append(remote(my_total, z_total.at[i], tzs.at[i], tzr.at[i], peer))
        copies.append(remote(all_cot.at[tile], all_cot.at[tile], zs.at[i], zr.at[i], peer))
    for copy in copies:
        copy.start()
    for i in range(sz.nz - 1):
        source = x * sz.nz + (z + sz.nz - 1 - i) % sz.nz
        remote(my_total, z_total.at[i], tzs.at[i], tzr.at[i], z_peers[i]).wait_recv()
        remote(all_cot.at[tile], all_cot.at[source], zs.at[i], zr.at[i], z_peers[i]).wait_recv()
        mine = mine + z_total[i]
    total[...] = mine
    later = []
    for i, peer in enumerate(x_peers):
        block = all_cot.at[pl.ds(x * sz.nz, sz.nz)]
        later.append(remote(total, x_total.at[i], txs.at[i], txr.at[i], peer))
        later.append(remote(block, block, xs.at[i], xr.at[i], peer))
    for copy in later:
        copy.start()
    for i in range(sz.nx - 1):
        source = (x + sz.nx - 1 - i) % sz.nx
        remote(total, x_total.at[i], txs.at[i], txr.at[i], x_peers[i]).wait_recv()
        block = all_cot.at[pl.ds(source * sz.nz, sz.nz)]
        remote(block, block, xs.at[i], xr.at[i], x_peers[i]).wait_recv()
        mine = mine + x_total[i]
    for copy in copies + later:
        copy.wait_send()

    denominator = jnp.maximum(mine, 1.0)

    def pick(owner):
        found = jnp.sum(jnp.where(lane == owner, denominator, 0.0), axis=1, keepdims=True)
        return jnp.broadcast_to(found[0:1], (sz.pairs, LANES))

    den_out[...] = pick(tile)
    for s, (coef, target) in enumerate(routes):
        scaled = (LOSS_SCALE * all_cot[target].astype(f32) / pick(target)).astype(bf16)
        grad_out[s] = coef * scaled.astype(f32)


def compute_kernel(
    sz, counts, weights, slide_of, owner_map, tiles, weight, grad, input_grad, terms, parts,
    xp, gp, xc, gc, w_rows, w_lanes,
):
    pair = pl.program_id(0)

    @pl.when(pair == 0)
    def _():
        xp[...] = jnp.zeros_like(xp)
        gp[...] = jnp.zeros_like(gp)

    low = lax.broadcasted_iota(jnp.int32, (WIDTH, LANES), 1) < WIDTH
    for tap in range(TAPS):
        w = weight[tap]
        zero = jnp.zeros_like(w)
        first, second = jnp.where(low, w, zero), jnp.where(low, zero, w)
        w_rows[pl.ds(tap * LANES, WIDTH), :] = first
        w_rows[pl.ds(tap * LANES + WIDTH, WIDTH), :] = second
        w_lanes[pl.ds(0, WIDTH), pl.ds(tap * LANES, LANES)] = first
        w_lanes[pl.ds(WIDTH, WIDTH), pl.ds(tap * LANES, LANES)] = second
    for t in range(SLOTS):
        for h in range(SIDE):
            xp[pl.ds(BASE + 64 * t + 8 * h, SIDE), :] = tiles[0, t, h].astype(f32)
    for tap in range(TAPS):
        shift = 8 * (tap // 3 - 1) + tap % 3 - 1
        xc[:, pl.ds(tap * LANES, LANES)] = xp[pl.ds(BASE + shift, ROWS), :].astype(bf16)
    pre = jnp.dot(xc[...], w_rows[...], preferred_element_type=f32)
    sigma = 1.0 / (1.0 + jnp.exp(-pre))
    row = lax.broadcasted_iota(jnp.int32, (64, LANES), 0)
    real = (row % 8 < SIDE) & (row < 8 * SIDE)
    owner = lax.broadcasted_iota(jnp.int32, (sz.tiles, LANES), 0)
    part = jnp.zeros((sz.tiles, LANES), f32)
    pieces = []
    for t in range(SLOTS):
        v, q = pre[64 * t : 64 * t + 64], sigma[64 * t : 64 * t + 64]
        mean = jnp.sum(jnp.where(real, v * q, 0.0), axis=0, keepdims=True) / (SIDE * SIDE)
        embedding = mean.astype(bf16).astype(f32)
        coef, target = slot_route(t, counts, weights, slide_of, owner_map)
        part = part + jnp.where(owner == target, coef, 0.0) * embedding
        slope = q * (1.0 + v * (1.0 - q))
        upstream = grad[t, pl.ds(pair, 1), :] / (SIDE * SIDE)
        pieces.append(jnp.where(real, upstream * slope, 0.0))
    parts[:, pl.ds(pair, 1), :] = part.reshape(sz.tiles, 1, LANES)
    g = jnp.concatenate(pieces, axis=0)
    gp[pl.ds(BASE, ROWS), :] = g
    for tap in range(TAPS):
        shift = 8 * (tap // 3 - 1) + tap % 3 - 1
        gc[:, pl.ds(tap * LANES, LANES)] = gp[pl.ds(BASE - shift, ROWS), :].astype(bf16)
    dx = lax.dot_general(gc[...], w_lanes[...], (((1,), (1,)), ((), ())), preferred_element_type=f32)
    for t in range(SLOTS):
        for h in range(SIDE):
            at = 64 * t + 8 * h
            input_grad[0, t, h] = dx[at : at + SIDE]
    dw = jnp.dot(g.astype(bf16).T, xc[...], preferred_element_type=f32)
    low = lax.broadcasted_iota(jnp.int32, (32, LANES), 1) < WIDTH
    for tap in range(TAPS):
        d = dw[:, tap * LANES : (tap + 1) * LANES]
        even = jnp.where(low, d[0:32], pltpu.roll(d[32:64], WIDTH, 1))
        odd = jnp.where(low, pltpu.roll(d[64:96], WIDTH, 1), d[96:128])
        terms[0, 0, pl.ds(tap * 32, 32), :] = even.astype(bf16)
        terms[1, 0, pl.ds(tap * 32, 32), :] = odd.astype(bf16)


def reduce_kernel(
    sz, terms, parts, den, pooled, result,
    c_in, s1, y_in, s2, x_in, s3f, s3, z_in, own, fin, px_in, psum, pz_in,
    cs, cr, ys, yr, xs, xr, zs, zr, fs, fr, pxs, pxr, pzs, pzr,
):
    tile, slide, x, z, y, c = position(sz)
    nx, ny, nz = sz.nx, sz.ny, sz.nz
    mate = (tile, y * 2 + 1 - c)
    y_peers = [(tile, ((y + off) % ny) * 2 + c) for off in range(1, ny)]
    x_peers = [(((x + off) % nx) * nz + z, slide) for off in range(1, nx)]
    z_peers = [(x * nz + (z + off) % nz, slide) for off in range(1, nz)]
    home = y * nz + 2 * x + c
    at_home = home == tile
    homes = [(home, (slide + d) % sz.slides) for d in range(sz.slides)]
    source_slide = x * 2 + z % 2
    sources = [((z // 2) * nz + q, source_slide) for q in range(nz)]
    symmetric = [mate] + y_peers + x_peers + z_peers
    for peer in symmetric:
        signal(peer)
    for q in range(nz):

        @pl.when(jnp.logical_not(at_home & (z == q)))
        def _():
            signal(sources[q])

    pl.semaphore_wait(
        pltpu.get_barrier_semaphore(), len(symmetric) + sz.slides - at_home.astype(jnp.int32)
    )
    started = []

    def start(copy):
        copy.start()
        started.append(copy)
        return copy

    p_copies = []
    for i, peer in enumerate(x_peers):
        xo = (x + i + 1) % nx
        p_copies.append(start(remote(parts.at[pl.ds(xo * nz, nz)], px_in.at[i], pxs.at[i], pxr.at[i], peer)))
    order = list(range(1, ny)) + [0]
    c_copies = []
    for i, off in enumerate(order):
        block = pl.ds(((y + off) % ny) * nx, nx)
        c_copies.append(start(remote(terms.at[1 - c, block], c_in.at[block], cs.at[i], cr.at[i], mate)))
    y_copies = []
    for i, off in enumerate(order):
        first = ((y + off) % ny) * nx
        c_copies[i].wait_recv()

        @pl.loop(0, nx)
        def _(k):
            s1[first + k] = (terms[c, first + k].astype(f32) + c_in[first + k].astype(f32)).astype(bf16)

        if off:
            y_copies.append(start(remote(s1.at[pl.ds(first, nx)], y_in.at[off - 1], ys.at[off - 1], yr.at[off - 1], y_peers[off - 1])))
    for copy in p_copies:
        copy.wait_recv()

    @pl.loop(0, nz)
    def _(k):
        v = parts[x * nz + k]
        for i in range(nx - 1):
            v = v + px_in[i, k]
        psum[k] = v

    pz_copies = []
    for i, peer in enumerate(z_peers):
        pz_copies.append(start(remote(psum.at[(z + i + 1) % nz], pz_in.at[i], pzs.at[i], pzr.at[i], peer)))
    for copy in y_copies:
        copy.wait_recv()

    @pl.loop(0, nx)
    def _(k):
        v = s1[y * nx + k].astype(f32)
        for i in range(ny - 1):
            v = v + y_in[i, k].astype(f32)
        s2[k] = v.astype(bf16)

    x_copies = []
    for i, peer in enumerate(x_peers):
        x_copies.append(start(remote(s2.at[(x + i + 1) % nx], x_in.at[i], xs.at[i], xr.at[i], peer)))
    for copy in x_copies:
        copy.wait_recv()
    v = s2[x].astype(f32)
    for i in range(nx - 1):
        v = v + x_in[i].astype(f32)
    s3f[...] = v
    for q in range(nz):
        s3[q, pl.ds(0, sz.piece), :] = s3f[pl.ds(q * sz.piece, sz.piece), :].astype(bf16)
    z_copies = []
    for i, peer in enumerate(z_peers):
        z_copies.append(start(remote(s3.at[(z + i + 1) % nz], z_in.at[i], zs.at[i], zr.at[i], peer)))
    for copy in z_copies:
        copy.wait_recv()
    v = s3[z, pl.ds(0, sz.piece), :].astype(f32)
    for i in range(nz - 1):
        v = v + z_in[i, pl.ds(0, sz.piece), :].astype(f32)
    own[pl.ds(0, sz.piece), :] = v / LOSS_SCALE
    for d, peer in enumerate(homes):
        copy = remote(own, fin.at[z], fs.at[d], fr.at[z], peer)
        if d == 0:

            @pl.when(jnp.logical_not(at_home))
            def _():
                copy.start()

        else:
            start(copy)

    @pl.when(at_home)
    def _():
        fin[z] = own[...]

    for copy in pz_copies:
        copy.wait_recv()
    v = psum[z]
    for i in range(nz - 1):
        v = v + pz_in[i]
    pooled[...] = v / den[...]
    for q in range(nz):

        @pl.when(jnp.logical_not(at_home & (z == q)))
        def _():
            remote(own, fin.at[q], fs.at[0], fr.at[q], sources[q]).wait_recv()

    for q in range(nz):
        result[pl.ds(q * sz.piece, sz.piece), :] = fin[q, pl.ds(0, sz.piece), :]

    @pl.when(jnp.logical_not(at_home))
    def _():
        remote(own, fin.at[z], fs.at[0], fr.at[z], homes[0]).wait_send()

    for copy in started:
        copy.wait_send()


def shards(sz, tiles, counts, weights, slide_of, owner_map, cot, conv_weight):
    pairs, channels = sz.pairs, sz.tiles * WIDTH
    smem = pl.BlockSpec(memory_space=pltpu.SMEM)
    vmem = pl.BlockSpec(memory_space=pltpu.VMEM)
    dma = pltpu.SemaphoreType.DMA
    routing = (counts, weights, slide_of, owner_map)
    grad, den = pl.pallas_call(
        functools.partial(gather_kernel, sz),
        out_shape=(
            jax.ShapeDtypeStruct((SLOTS, pairs, LANES), f32),
            jax.ShapeDtypeStruct((pairs, LANES), f32),
        ),
        in_specs=[smem] * 4 + [vmem],
        out_specs=(vmem, vmem),
        scratch_shapes=[
            pltpu.VMEM((pairs, LANES), f32),
            pltpu.VMEM((sz.tiles, pairs, LANES), bf16),
            pltpu.VMEM((8, LANES), f32),
            pltpu.VMEM((sz.nz - 1, 8, LANES), f32),
            pltpu.VMEM((sz.nx - 1, 8, LANES), f32),
            pltpu.VMEM((8, LANES), f32),
        ]
        + [dma((sz.nz - 1,))] * 2
        + [dma((sz.nx - 1,))] * 2
        + [dma((sz.nz - 1,))] * 2
        + [dma((sz.nx - 1,))] * 2,
        compiler_params=pltpu.CompilerParams(collective_id=0, has_side_effects=True),
        name="gather",
    )(*routing, cot)

    input_grad, terms, parts = pl.pallas_call(
        functools.partial(compute_kernel, sz),
        grid=(pairs,),
        out_shape=(
            jax.ShapeDtypeStruct((1, SLOTS, SIDE, SIDE, channels), f32),
            jax.ShapeDtypeStruct((2, pairs, PACKED, LANES), bf16),
            jax.ShapeDtypeStruct((sz.tiles, pairs, LANES), f32),
        ),
        in_specs=[smem] * 4
        + [
            pl.BlockSpec((1, SLOTS, SIDE, SIDE, LANES), lambda p: (0, 0, 0, 0, p)),
            pl.BlockSpec((TAPS, WIDTH, LANES), lambda p: (0, 0, p)),
            vmem,
        ],
        out_specs=(
            pl.BlockSpec((1, SLOTS, SIDE, SIDE, LANES), lambda p: (0, 0, 0, 0, p)),
            pl.BlockSpec((2, 1, PACKED, LANES), lambda p: (0, p, 0, 0)),
            pl.BlockSpec((sz.tiles, pairs, LANES), lambda p: (0, 0, 0)),
        ),
        scratch_shapes=[
            pltpu.VMEM((PADDED, LANES), f32),
            pltpu.VMEM((PADDED, LANES), f32),
            pltpu.VMEM((ROWS, TAPS * LANES), bf16),
            pltpu.VMEM((ROWS, TAPS * LANES), bf16),
            pltpu.VMEM((TAPS * LANES, LANES), bf16),
            pltpu.VMEM((LANES, TAPS * LANES), bf16),
        ],
        compiler_params=pltpu.CompilerParams(
            dimension_semantics=("arbitrary",), vmem_limit_bytes=40 * 1024 * 1024
        ),
        name="compute",
    )(*routing, tiles, conv_weight, grad)

    piece_pad = (sz.piece + 15) // 16 * 16
    pooled, result = pl.pallas_call(
        functools.partial(reduce_kernel, sz),
        out_shape=(
            jax.ShapeDtypeStruct((pairs, LANES), f32),
            jax.ShapeDtypeStruct((PACKED, LANES), f32),
        ),
        in_specs=[vmem] * 3,
        out_specs=(vmem, vmem),
        scratch_shapes=[
            pltpu.VMEM((pairs, PACKED, LANES), bf16),
            pltpu.VMEM((pairs, PACKED, LANES), bf16),
            pltpu.VMEM((sz.ny - 1, sz.nx, PACKED, LANES), bf16),
            pltpu.VMEM((sz.nx, PACKED, LANES), bf16),
            pltpu.VMEM((sz.nx - 1, PACKED, LANES), bf16),
            pltpu.VMEM((PACKED, LANES), f32),
            pltpu.VMEM((sz.nz, piece_pad, LANES), bf16),
            pltpu.VMEM((sz.nz - 1, piece_pad, LANES), bf16),
            pltpu.VMEM((piece_pad, LANES), f32),
            pltpu.VMEM((sz.nz, piece_pad, LANES), f32),
            pltpu.VMEM((sz.nx - 1, sz.nz, pairs, LANES), f32),
            pltpu.VMEM((sz.nz, pairs, LANES), f32),
            pltpu.VMEM((sz.nz - 1, pairs, LANES), f32),
        ]
        + [dma((sz.ny,))] * 2
        + [dma((sz.ny - 1,))] * 2
        + [dma((sz.nx - 1,))] * 2
        + [dma((sz.nz - 1,))] * 2
        + [dma((sz.slides,)), dma((sz.nz,))]
        + [dma((sz.nx - 1,))] * 2
        + [dma((sz.nz - 1,))] * 2,
        compiler_params=pltpu.CompilerParams(
            collective_id=1, has_side_effects=True, vmem_limit_bytes=40 * 1024 * 1024
        ),
        name="reduce",
    )(terms, parts, den)
    weight_grad = result.reshape(TAPS, 32, 2, WIDTH).transpose(0, 3, 2, 1).reshape(TAPS, WIDTH, WIDTH)
    return pooled.reshape(1, 1, channels), input_grad, weight_grad


def solution(mesh):
    sz = Sizes(mesh)
    return jax.shard_map(
        functools.partial(shards, sz),
        mesh=mesh,
        in_specs=(
            P("slide", "tile", None, None, None),
            P("slide", "tile"),
            P("slide", "tile"),
            P("slide", "tile", None),
            P("slide", None),
            P("slide", "tile", None),
            P(),
        ),
        out_specs=(
            P("slide", "tile", None),
            P("slide", "tile", None, None, None),
            P(None, None, "tile"),
        ),
        check_vma=False,
    )
```

```python
import functools

import jax
import jax.numpy as jnp
from jax import lax
from jax.experimental import pallas as pl
from jax.experimental.pallas import tpu as pltpu
from jax.sharding import PartitionSpec as P

MESH = pl.DeviceIdType.MESH
LOSS_SCALE = 512.0
SIDE = 7
SLOTS = 3
WIDTH = 64
LANES = 128
TAPS = 9
ROWS = SLOTS * 64
BASE = 16
PADDED = BASE + ROWS + 16
f32 = jnp.float32
bf16 = jnp.bfloat16


class Sizes:
    def __init__(self, mesh):
        self.tiles = mesh.shape["tile"]
        self.slides = mesh.shape["slide"]
        self.ny = self.slides // 2
        self.nx = self.ny
        self.nz = self.tiles // self.nx
        self.pairs = self.tiles // 2
        self.share = 32 // self.ny
        self.packed = TAPS * self.share
        self.packed_pad = (self.packed + 15) // 16 * 16


def position(sz):
    tile = lax.axis_index("tile")
    slide = lax.axis_index("slide")
    return tile, slide, tile // sz.nz, tile % sz.nz, slide // 2, slide % 2


def remote(src, dst, send, recv, device):
    return pltpu.make_async_remote_copy(
        src_ref=src, dst_ref=dst, send_sem=send, recv_sem=recv, device_id=device, device_id_type=MESH
    )


def signal(device):
    pl.semaphore_signal(pltpu.get_barrier_semaphore(), inc=1, device_id=device, device_id_type=MESH)


def slot_route(slot, counts, weights, slide_of, owner_map):
    coef = jnp.where(slot < counts[0, 0], weights[0, slot], 0.0)
    return coef, owner_map[0, slide_of[0, slot]]


C_LAG = 2
Y_LAG = 5
BARRIER_STEP = 1
Z_STEP = 6
P_STEP = 5


def fused_kernel(
    sz, counts, weights, slide_of, owner_map, cot, tiles_hbm, weight_hbm,
    pooled, input_grad, result,
    tiles, weight, stage, all_cot, my_total, z_total, x_total, total, grad,
    xp, gp, xc, gc, w_rows, w_lanes, slopes, parts,
    terms, c_in, s1, y_in, s2, o_in, own, fin, px_in, psum, pz_in,
    tile_sem, weight_sem, gzs, gzr, gxs, gxr, tzs, tzr, txs, txr,
    cs, cr, ys, yr, os, orr, fs, fr, pxs, pxr, pzs, pzr,
):
    tile, slide, x, z, y, c = position(sz)
    nx, ny, nz, pairs = sz.nx, sz.ny, sz.nz, sz.pairs
    share, packed = sz.share, sz.packed
    z_peers = [(x * nz + (z + off) % nz, slide) for off in range(1, nz)]
    x_peers = [(((x + off) % nx) * nz + z, slide) for off in range(1, nx)]
    mate = (tile, y * 2 + 1 - c)
    y_peers = [(tile, ((y + off) % ny) * 2 + c) for off in range(1, ny)]
    is_owner = (z % 2) == c

    def pair_at(s):
        return (tile // 2 + 1 + s) % pairs

    def lanes_of(s):
        return pl.ds(pl.multiple_of(pair_at(s) * LANES, LANES), LANES)

    def load(s):
        lanes = lanes_of(s)
        return (
            pltpu.make_async_copy(tiles_hbm.at[0, :, :, :, lanes], tiles.at[s], tile_sem.at[s]),
            pltpu.make_async_copy(weight_hbm.at[:, :, lanes], weight.at[s], weight_sem.at[s]),
        )

    @pl.loop(0, pairs)
    def _(s):
        for copy in load(s):
            copy.start()

    @pl.loop(1, sz.tiles)
    def _(d):
        signal(((tile + d) % sz.tiles, slide))

    @pl.loop(1, sz.slides)
    def _(d):
        signal((tile, (slide + d) % sz.slides))

    xp[...] = jnp.zeros_like(xp)
    gp[...] = jnp.zeros_like(gp)
    for j in range(pairs):
        stage[pl.ds(j, 1), :] = cot[0, :, pl.ds(j * LANES, LANES)].astype(f32)
    all_cot[tile] = stage[...].astype(bf16)
    lane = lax.broadcasted_iota(jnp.int32, (8, LANES), 1)
    routes = [slot_route(s, counts, weights, slide_of, owner_map) for s in range(SLOTS)]
    mine = jnp.zeros((8, LANES), f32)
    for coef, target in routes:
        mine = mine + jnp.where(lane == target, coef, 0.0)
    my_total[...] = mine

    def total_z(i):
        return remote(my_total, z_total.at[i], tzs.at[i], tzr.at[i], z_peers[i])

    def rows_z(i, source):
        return remote(all_cot.at[source], all_cot.at[source], gzs.at[i], gzr.at[i], z_peers[i])

    def total_x(i):
        return remote(total, x_total.at[i], txs.at[i], txr.at[i], x_peers[i])

    def rows_x(i, source):
        block = all_cot.at[pl.ds(source * nz, nz)]
        return remote(block, block, gxs.at[i], gxr.at[i], x_peers[i])

    low64 = lax.broadcasted_iota(jnp.int32, (WIDTH, LANES), 1) < WIDTH
    row = lax.broadcasted_iota(jnp.int32, (64, LANES), 0)
    real = (row % 8 < SIDE) & (row < 8 * SIDE)
    owner_row = lax.broadcasted_iota(jnp.int32, (sz.tiles, LANES), 0)

    @pl.loop(0, pairs)
    def _(s):
        @pl.when(s == BARRIER_STEP)
        def _():
            pl.semaphore_wait(pltpu.get_barrier_semaphore(), sz.tiles + sz.slides - 2)
            for i in range(nz - 1):
                total_z(i).start()
                rows_z(i, tile).start()

        @pl.when(s == min(Z_STEP, pairs - 1))
        def _():
            v = my_total[...]
            for i in range(nz - 1):
                total_z(i).wait_recv()
                rows_z(i, x * nz + (z + nz - 1 - i) % nz).wait_recv()
                v = v + z_total[i]
            total[...] = v
            for i in range(nx - 1):
                total_x(i).start()
                rows_x(i, x).start()

        for copy in load(s):
            copy.wait()
        for tap in range(TAPS):
            w = weight[s, tap]
            zero = jnp.zeros_like(w)
            first, second = jnp.where(low64, w, zero), jnp.where(low64, zero, w)
            w_rows[pl.ds(tap * LANES, WIDTH), :] = first
            w_rows[pl.ds(tap * LANES + WIDTH, WIDTH), :] = second
            w_lanes[s, pl.ds(0, WIDTH), pl.ds(tap * LANES, LANES)] = first
            w_lanes[s, pl.ds(WIDTH, WIDTH), pl.ds(tap * LANES, LANES)] = second
        for t in range(SLOTS):
            for h in range(SIDE):
                xp[pl.ds(BASE + 64 * t + 8 * h, SIDE), :] = tiles[s, t, h].astype(f32)
        for tap in range(TAPS):
            shift = 8 * (tap // 3 - 1) + tap % 3 - 1
            xc[s, :, pl.ds(tap * LANES, LANES)] = xp[pl.ds(BASE + shift, ROWS), :].astype(bf16)
        pre = jnp.dot(xc[s], w_rows[...], preferred_element_type=f32)
        sigma = 1.0 / (1.0 + jnp.exp(-pre))
        part = jnp.zeros((sz.tiles, LANES), f32)
        for t in range(SLOTS):
            v, q = pre[64 * t : 64 * t + 64], sigma[64 * t : 64 * t + 64]
            mean = jnp.sum(jnp.where(real, v * q, 0.0), axis=0, keepdims=True) / (SIDE * SIDE)
            embedding = mean.astype(bf16).astype(f32)
            coef, target = routes[t]
            part = part + jnp.where(owner_row == target, coef, 0.0) * embedding
            slope = q * (1.0 + v * (1.0 - q))
            slopes[s, pl.ds(64 * t, 64), :] = jnp.where(real, slope, 0.0)
        parts[:, pl.ds(pair_at(s), 1), :] = part.reshape(sz.tiles, 1, LANES)

    def parts_x(i):
        xo = (x + i + 1) % nx
        return remote(parts.at[pl.ds(xo * nz, nz)], px_in.at[i], pxs.at[i], pxr.at[i], x_peers[i])

    def parts_z(i):
        return remote(psum.at[(z + i + 1) % nz], pz_in.at[i], pzs.at[i], pzr.at[i], z_peers[i])

    for i in range(nx - 1):
        parts_x(i).start()
    v = total[...]
    for i in range(nx - 1):
        total_x(i).wait_recv()
        rows_x(i, (x + nx - 1 - i) % nx).wait_recv()
        v = v + x_total[i]
    denominator = jnp.maximum(v, 1.0)

    def pick(owner):
        found = jnp.sum(jnp.where(lane == owner, denominator, 0.0), axis=1, keepdims=True)
        return jnp.broadcast_to(found[0:1], (pairs, LANES))

    for t, (coef, target) in enumerate(routes):
        scaled = (LOSS_SCALE * all_cot[target].astype(f32) / pick(target)).astype(bf16)
        grad[t] = coef * scaled.astype(f32)

    def swap(s):
        return remote(terms.at[1 - c, s], c_in.at[s], cs.at[s], cr.at[s], mate)

    def along_y(i, s):
        return remote(s1.at[s, (y + i + 1) % ny], y_in.at[i, s], ys.at[i, s], yr.at[i, s], y_peers[i])

    def to_owner(s):
        return remote(s2.at[s], o_in.at[tile], os.at[s], orr.at[tile], (2 * pair_at(s) + c, slide))

    low = lax.broadcasted_iota(jnp.int32, (32, LANES), 1) < WIDTH
    none = jnp.zeros((share, LANES), f32)

    @pl.loop(0, pairs + Y_LAG)
    def _(s):
        @pl.when(s < pairs)
        def _():
            for t in range(SLOTS):
                upstream = grad[t, pl.ds(pair_at(s), 1), :] / (SIDE * SIDE)
                gp[pl.ds(BASE + 64 * t, 64), :] = upstream * slopes[s, pl.ds(64 * t, 64), :]
            g = gp[pl.ds(BASE, ROWS), :].astype(bf16)
            dw = jnp.dot(g.T, xc[s], preferred_element_type=f32)
            even, odd = [], []
            for tap in range(TAPS):
                d = dw[:, tap * LANES : (tap + 1) * LANES]
                even.append(jnp.where(low, d[0:32], pltpu.roll(d[32:64], WIDTH, 1)))
                odd.append(jnp.where(low, pltpu.roll(d[64:96], WIDTH, 1), d[96:128]))
            per = 16 // share
            for parity, rows in enumerate((even, odd)):
                for yy in range(ny):
                    for j in range(sz.packed_pad // 16):
                        block = [
                            rows[tap][yy * share : (yy + 1) * share] if tap < TAPS else none
                            for tap in range(j * per, (j + 1) * per)
                        ]
                        terms[parity, s, yy, pl.ds(16 * j, 16), :] = jnp.concatenate(block, axis=0).astype(bf16)
            swap(s).start()
            for tap in range(TAPS):
                shift = 8 * (tap // 3 - 1) + tap % 3 - 1
                gc[:, pl.ds(tap * LANES, LANES)] = gp[pl.ds(BASE - shift, ROWS), :].astype(bf16)
            dx = lax.dot_general(
                gc[...], w_lanes[s], (((1,), (1,)), ((), ())), preferred_element_type=f32
            )
            lanes = lanes_of(s)
            for t in range(SLOTS):
                for h in range(SIDE):
                    at = 64 * t + 8 * h
                    input_grad[0, t, h, :, lanes] = dx[at : at + SIDE]

        @pl.when((s >= C_LAG) & (s < pairs + C_LAG))
        def _():
            r = s - C_LAG
            swap(r).wait_recv()
            s1[r] = (terms[c, r].astype(f32) + c_in[r].astype(f32)).astype(bf16)
            for i in range(ny - 1):
                along_y(i, r).start()

        @pl.when(s >= Y_LAG)
        def _():
            r = s - Y_LAG
            v = s1[r, y].astype(f32)
            for i in range(ny - 1):
                along_y(i, r).wait_recv()
                v = v + y_in[i, r].astype(f32)
            s2[r] = v.astype(bf16)

            @pl.when(2 * pair_at(r) + c != tile)
            def _():
                to_owner(r).start()

        @pl.when(s == P_STEP)
        def _():
            for i in range(nx - 1):
                parts_x(i).wait_recv()

            @pl.loop(0, nz)
            def _(k):
                v = parts[x * nz + k]
                for i in range(nx - 1):
                    v = v + px_in[i, k]
                psum[k] = v

            for i in range(nz - 1):
                parts_z(i).start()

    v = psum[z]
    for i in range(nz - 1):
        parts_z(i).wait_recv()
        v = v + pz_in[i]
    pooled[...] = v / pick(tile)

    finals = [(tile, (slide + d) % sz.slides) for d in range(1, sz.slides)]

    @pl.when(is_owner)
    def _():
        own[...] = s2[pairs - 1].astype(f32)

        @pl.loop(1, sz.tiles)
        def _(d):
            source = ((tile // 2) * 2 + sz.tiles - d) % sz.tiles
            source = source + (d // (sz.tiles - 1)) * ((tile // 2) * 2 + 1 - z % 2 - source)
            remote(s2.at[0], o_in.at[source], os.at[0], orr.at[source], mate).wait_recv()
            own[...] += o_in[source].astype(f32)

        own[...] = own[...] / LOSS_SCALE
        for d, peer in enumerate(finals):
            remote(own, fin.at[y], fs.at[d], fr.at[y], peer).start()
        fin[y] = own[...]

    for q in range(ny):

        @pl.when(jnp.logical_not(is_owner & (y == q)))
        def _():
            remote(own, fin.at[q], fs.at[0], fr.at[q], finals[0]).wait_recv()

    for tap in range(TAPS):
        rows = [fin[q, pl.ds(tap * share, share), :] for q in range(ny)]
        block = jnp.concatenate(rows, axis=0).T
        result[tap] = jnp.concatenate([block[0:WIDTH], block[WIDTH:]], axis=1)

    @pl.when(is_owner)
    def _():
        for d, peer in enumerate(finals):
            remote(own, fin.at[y], fs.at[d], fr.at[y], peer).wait_send()

    for i in range(nz - 1):
        total_z(i).wait_send()
        rows_z(i, tile).wait_send()
        parts_z(i).wait_send()
    for i in range(nx - 1):
        total_x(i).wait_send()
        rows_x(i, x).wait_send()
        parts_x(i).wait_send()

    @pl.loop(0, pairs)
    def _(s):
        swap(s).wait_send()
        for i in range(ny - 1):
            along_y(i, s).wait_send()

        @pl.when(2 * pair_at(s) + c != tile)
        def _():
            to_owner(s).wait_send()


def shards(sz, tiles, counts, weights, slide_of, owner_map, cot, conv_weight):
    pairs, channels = sz.pairs, sz.tiles * WIDTH
    smem = pl.BlockSpec(memory_space=pltpu.SMEM)
    vmem = pl.BlockSpec(memory_space=pltpu.VMEM)
    hbm = pl.BlockSpec(memory_space=pltpu.MemorySpace.HBM)
    dma = pltpu.SemaphoreType.DMA
    pad = sz.packed_pad
    pooled, input_grad, weight_grad = pl.pallas_call(
        functools.partial(fused_kernel, sz),
        out_shape=(
            jax.ShapeDtypeStruct((pairs, LANES), f32),
            jax.ShapeDtypeStruct((1, SLOTS, SIDE, SIDE, channels), f32),
            jax.ShapeDtypeStruct((TAPS, WIDTH, WIDTH), f32),
        ),
        in_specs=[smem] * 4 + [vmem] + [hbm] * 2,
        out_specs=(vmem, vmem, vmem),
        scratch_shapes=[
            pltpu.VMEM((pairs, SLOTS, SIDE, SIDE, LANES), bf16),
            pltpu.VMEM((pairs, TAPS, WIDTH, LANES), bf16),
            pltpu.VMEM((pairs, LANES), f32),
            pltpu.VMEM((sz.tiles, pairs, LANES), bf16),
            pltpu.VMEM((8, LANES), f32),
            pltpu.VMEM((sz.nz - 1, 8, LANES), f32),
            pltpu.VMEM((sz.nx - 1, 8, LANES), f32),
            pltpu.VMEM((8, LANES), f32),
            pltpu.VMEM((SLOTS, pairs, LANES), f32),
            pltpu.VMEM((PADDED, LANES), f32),
            pltpu.VMEM((PADDED, LANES), f32),
            pltpu.VMEM((pairs, ROWS, TAPS * LANES), bf16),
            pltpu.VMEM((ROWS, TAPS * LANES), bf16),
            pltpu.VMEM((TAPS * LANES, LANES), bf16),
            pltpu.VMEM((pairs, LANES, TAPS * LANES), bf16),
            pltpu.VMEM((pairs, ROWS, LANES), f32),
            pltpu.VMEM((sz.tiles, pairs, LANES), f32),
            pltpu.VMEM((2, pairs, sz.ny, pad, LANES), bf16),
            pltpu.VMEM((pairs, sz.ny, pad, LANES), bf16),
            pltpu.VMEM((pairs, sz.ny, pad, LANES), bf16),
            pltpu.VMEM((sz.ny - 1, pairs, pad, LANES), bf16),
            pltpu.VMEM((pairs, pad, LANES), bf16),
            pltpu.VMEM((sz.tiles, pad, LANES), bf16),
            pltpu.VMEM((pad, LANES), f32),
            pltpu.VMEM((sz.ny, pad, LANES), f32),
            pltpu.VMEM((sz.nx - 1, sz.nz, pairs, LANES), f32),
            pltpu.VMEM((sz.nz, pairs, LANES), f32),
            pltpu.VMEM((sz.nz - 1, pairs, LANES), f32),
        ]
        + [dma((pairs,))] * 2
        + [dma((sz.nz - 1,))] * 2
        + [dma((sz.nx - 1,))] * 2
        + [dma((sz.nz - 1,))] * 2
        + [dma((sz.nx - 1,))] * 2
        + [dma((pairs,))] * 2
        + [dma((sz.ny - 1, pairs))] * 2
        + [dma((pairs,)), dma((sz.tiles,))]
        + [dma((sz.slides,)), dma((sz.ny,))]
        + [dma((sz.nx - 1,))] * 2
        + [dma((sz.nz - 1,))] * 2,
        compiler_params=pltpu.CompilerParams(
            collective_id=0, has_side_effects=True, vmem_limit_bytes=56 * 1024 * 1024
        ),
        name="fused",
    )(counts, weights, slide_of[:, :, 0], owner_map, cot, tiles, conv_weight)
    return pooled.reshape(1, 1, channels), input_grad, weight_grad


def solution(mesh):
    sz = Sizes(mesh)
    return jax.shard_map(
        functools.partial(shards, sz),
        mesh=mesh,
        in_specs=(
            P("slide", "tile", None, None, None),
            P("slide", "tile"),
            P("slide", "tile"),
            P("slide", "tile", None),
            P("slide", None),
            P("slide", "tile", None),
            P(),
        ),
        out_specs=(
            P("slide", "tile", None),
            P("slide", "tile", None, None, None),
            P(None, None, "tile"),
        ),
        check_vma=False,
    )
```

```python
import functools

import jax
import jax.numpy as jnp
from jax import lax
from jax.experimental import pallas as pl
from jax.experimental.pallas import tpu as pltpu
from jax.sharding import PartitionSpec as P

MESH = pl.DeviceIdType.MESH
LOSS_SCALE = 512.0
SIDE = 7
SLOTS = 3
WIDTH = 64
LANES = 128
TAPS = 9
ROWS = SLOTS * 64
BASE = 16
PADDED = BASE + ROWS + 16
f32 = jnp.float32
bf16 = jnp.bfloat16


class Sizes:
    def __init__(self, mesh):
        self.tiles = mesh.shape["tile"]
        self.slides = mesh.shape["slide"]
        self.ny = self.slides // 2
        self.nx = self.ny
        self.nz = self.tiles // self.nx
        self.pairs = self.tiles // 2
        self.share = 32 // self.ny
        self.packed = TAPS * self.share
        self.packed_pad = (self.packed + 15) // 16 * 16


def position(sz):
    tile = lax.axis_index("tile")
    slide = lax.axis_index("slide")
    return tile, slide, tile // sz.nz, tile % sz.nz, slide // 2, slide % 2


def remote(src, dst, send, recv, device):
    return pltpu.make_async_remote_copy(
        src_ref=src, dst_ref=dst, send_sem=send, recv_sem=recv, device_id=device, device_id_type=MESH
    )


def signal(device):
    pl.semaphore_signal(pltpu.get_barrier_semaphore(), inc=1, device_id=device, device_id_type=MESH)


def slot_route(slot, counts, weights, slide_of, owner_map):
    coef = jnp.where(slot < counts[0, 0], weights[0, slot], 0.0)
    return coef, owner_map[0, slide_of[0, slot]]


C_LAG = 4
Y_LAG = 9
X_LAG = 9
BARRIER_STEP = 1
Z_STEP = 6
P_STEP = 5


def fused_kernel(
    sz, counts, weights, slide_of, owner_map, cot, tiles_hbm, weight_hbm,
    pooled, input_grad, result,
    tiles, weight, stage, all_cot, my_total, z_total, x_total, total, grad,
    xp, gp, xc, gc, w_rows, w_lanes, slopes, parts,
    terms, c_in, s1, y_in, s2, o_in, own, final, fin, px_in, psum, pz_in,
    tile_sem, weight_sem, gzs, gzr, gxs, gxr, tzs, tzr, txs, txr,
    cs, cr, ys, yr, os, orr, fs, fr, pxs, pxr, pzs, pzr,
):
    tile, slide, x, z, y, c = position(sz)
    nx, ny, nz, pairs = sz.nx, sz.ny, sz.nz, sz.pairs
    share, packed = sz.share, sz.packed
    z_peers = [(x * nz + (z + off) % nz, slide) for off in range(1, nz)]
    x_peers = [(((x + off) % nx) * nz + z, slide) for off in range(1, nx)]
    mate = (tile, y * 2 + 1 - c)
    y_peers = [(tile, ((y + off) % ny) * 2 + c) for off in range(1, ny)]
    is_owner = (z % 2) == c

    def pair_at(s):
        return (tile // 2 + 1 + s) % pairs

    def lanes_of(s):
        return pl.ds(pl.multiple_of(pair_at(s) * LANES, LANES), LANES)

    def load(s):
        lanes = lanes_of(s)
        return (
            pltpu.make_async_copy(tiles_hbm.at[0, :, :, :, lanes], tiles.at[s], tile_sem.at[s]),
            pltpu.make_async_copy(weight_hbm.at[:, :, lanes], weight.at[s], weight_sem.at[s]),
        )

    @pl.loop(0, pairs)
    def _(s):
        for copy in load(s):
            copy.start()

    @pl.loop(1, sz.tiles)
    def _(d):
        signal(((tile + d) % sz.tiles, slide))

    @pl.loop(1, sz.slides)
    def _(d):
        signal((tile, (slide + d) % sz.slides))

    xp[...] = jnp.zeros_like(xp)
    gp[...] = jnp.zeros_like(gp)
    for j in range(pairs):
        stage[pl.ds(j, 1), :] = cot[0, :, pl.ds(j * LANES, LANES)].astype(f32)
    all_cot[tile] = stage[...].astype(bf16)
    lane = lax.broadcasted_iota(jnp.int32, (8, LANES), 1)
    routes = [slot_route(s, counts, weights, slide_of, owner_map) for s in range(SLOTS)]
    mine = jnp.zeros((8, LANES), f32)
    for coef, target in routes:
        mine = mine + jnp.where(lane == target, coef, 0.0)
    my_total[...] = mine

    def total_z(i):
        return remote(my_total, z_total.at[i], tzs.at[i], tzr.at[i], z_peers[i])

    def rows_z(i, source):
        return remote(all_cot.at[source], all_cot.at[source], gzs.at[i], gzr.at[i], z_peers[i])

    def total_x(i):
        return remote(total, x_total.at[i], txs.at[i], txr.at[i], x_peers[i])

    def rows_x(i, source):
        block = all_cot.at[pl.ds(source * nz, nz)]
        return remote(block, block, gxs.at[i], gxr.at[i], x_peers[i])

    low64 = lax.broadcasted_iota(jnp.int32, (WIDTH, LANES), 1) < WIDTH
    row = lax.broadcasted_iota(jnp.int32, (64, LANES), 0)
    real = (row % 8 < SIDE) & (row < 8 * SIDE)
    owner_row = lax.broadcasted_iota(jnp.int32, (sz.tiles, LANES), 0)

    @pl.loop(0, pairs)
    def _(s):
        @pl.when(s == BARRIER_STEP)
        def _():
            pl.semaphore_wait(pltpu.get_barrier_semaphore(), sz.tiles + sz.slides - 2)
            for i in range(nz - 1):
                total_z(i).start()
                rows_z(i, tile).start()

        @pl.when(s == min(Z_STEP, pairs - 1))
        def _():
            v = my_total[...]
            for i in range(nz - 1):
                total_z(i).wait_recv()
                rows_z(i, x * nz + (z + nz - 1 - i) % nz).wait_recv()
                v = v + z_total[i]
            total[...] = v
            for i in range(nx - 1):
                total_x(i).start()
                rows_x(i, x).start()

        for copy in load(s):
            copy.wait()
        for tap in range(TAPS):
            w = weight[s, tap]
            zero = jnp.zeros_like(w)
            first, second = jnp.where(low64, w, zero), jnp.where(low64, zero, w)
            w_rows[pl.ds(tap * LANES, WIDTH), :] = first
            w_rows[pl.ds(tap * LANES + WIDTH, WIDTH), :] = second
            w_lanes[s, pl.ds(0, WIDTH), pl.ds(tap * LANES, LANES)] = first
            w_lanes[s, pl.ds(WIDTH, WIDTH), pl.ds(tap * LANES, LANES)] = second
        for t in range(SLOTS):
            for h in range(SIDE):
                xp[pl.ds(BASE + 64 * t + 8 * h, SIDE), :] = tiles[s, t, h].astype(f32)
        for tap in range(TAPS):
            shift = 8 * (tap // 3 - 1) + tap % 3 - 1
            xc[s, :, pl.ds(tap * LANES, LANES)] = xp[pl.ds(BASE + shift, ROWS), :].astype(bf16)
        pre = jnp.dot(xc[s], w_rows[...], preferred_element_type=f32)
        sigma = 1.0 / (1.0 + jnp.exp(-pre))
        part = jnp.zeros((sz.tiles, LANES), f32)
        for t in range(SLOTS):
            v, q = pre[64 * t : 64 * t + 64], sigma[64 * t : 64 * t + 64]
            mean = jnp.sum(jnp.where(real, v * q, 0.0), axis=0, keepdims=True) / (SIDE * SIDE)
            embedding = mean.astype(bf16).astype(f32)
            coef, target = routes[t]
            part = part + jnp.where(owner_row == target, coef, 0.0) * embedding
            slope = q * (1.0 + v * (1.0 - q))
            slopes[s, pl.ds(64 * t, 64), :] = jnp.where(real, slope, 0.0)
        parts[:, pl.ds(pair_at(s), 1), :] = part.reshape(sz.tiles, 1, LANES)

    def parts_x(i):
        xo = (x + i + 1) % nx
        return remote(parts.at[pl.ds(xo * nz, nz)], px_in.at[i], pxs.at[i], pxr.at[i], x_peers[i])

    def parts_z(i):
        return remote(psum.at[(z + i + 1) % nz], pz_in.at[i], pzs.at[i], pzr.at[i], z_peers[i])

    for i in range(nx - 1):
        parts_x(i).start()
    v = total[...]
    for i in range(nx - 1):
        total_x(i).wait_recv()
        rows_x(i, (x + nx - 1 - i) % nx).wait_recv()
        v = v + x_total[i]
    denominator = jnp.maximum(v, 1.0)

    def pick(owner):
        found = jnp.sum(jnp.where(lane == owner, denominator, 0.0), axis=1, keepdims=True)
        return jnp.broadcast_to(found[0:1], (pairs, LANES))

    for t, (coef, target) in enumerate(routes):
        scaled = (LOSS_SCALE * all_cot[target].astype(f32) / pick(target)).astype(bf16)
        grad[t] = coef * scaled.astype(f32)

    def swap(s):
        return remote(terms.at[1 - c, s], c_in.at[s], cs.at[s], cr.at[s], mate)

    def along_y(i, s):
        return remote(s1.at[s, (y + i + 1) % ny], y_in.at[i, s], ys.at[i, s], yr.at[i, s], y_peers[i])

    def to_owner(s):
        return remote(s2.at[s], o_in.at[tile], os.at[s], orr.at[tile], (2 * pair_at(s) + c, slide))

    low = lax.broadcasted_iota(jnp.int32, (32, LANES), 1) < WIDTH
    none = jnp.zeros((share, LANES), f32)

    def pre_grad(s):
        upstream = [grad[t, pl.ds(pair_at(s), 1), :] / (SIDE * SIDE) for t in range(SLOTS)]
        return [upstream[t] * slopes[s, pl.ds(64 * t, 64), :] for t in range(SLOTS)]

    @pl.loop(0, pairs + Y_LAG)
    def _(s):
        @pl.when(s < pairs)
        def _():
            g = jnp.concatenate(pre_grad(s), axis=0).astype(bf16)
            dw = jnp.dot(g.T, xc[s], preferred_element_type=f32)
            even, odd = [], []
            for tap in range(TAPS):
                d = dw[:, tap * LANES : (tap + 1) * LANES]
                even.append(jnp.where(low, d[0:32], pltpu.roll(d[32:64], WIDTH, 1)))
                odd.append(jnp.where(low, pltpu.roll(d[64:96], WIDTH, 1), d[96:128]))
            per = 16 // share
            for parity, rows in enumerate((even, odd)):
                for yy in range(ny):
                    for j in range(sz.packed_pad // 16):
                        block = [
                            rows[tap][yy * share : (yy + 1) * share] if tap < TAPS else none
                            for tap in range(j * per, (j + 1) * per)
                        ]
                        terms[parity, s, yy, pl.ds(16 * j, 16), :] = jnp.concatenate(block, axis=0).astype(bf16)
            swap(s).start()

        @pl.when((s >= X_LAG) & (s < pairs + X_LAG))
        def _():
            r = s - X_LAG
            for t, rows in enumerate(pre_grad(r)):
                gp[pl.ds(BASE + 64 * t, 64), :] = rows
            for tap in range(TAPS):
                shift = 8 * (tap // 3 - 1) + tap % 3 - 1
                gc[:, pl.ds(tap * LANES, LANES)] = gp[pl.ds(BASE - shift, ROWS), :].astype(bf16)
            dx = lax.dot_general(
                gc[...], w_lanes[r], (((1,), (1,)), ((), ())), preferred_element_type=f32
            )
            lanes = lanes_of(r)
            for t in range(SLOTS):
                for h in range(SIDE):
                    at = 64 * t + 8 * h
                    input_grad[t, h, :, :, lanes] = dx[at : at + SIDE].reshape(SIDE, 1, LANES)

        @pl.when((s >= C_LAG) & (s < pairs + C_LAG))
        def _():
            r = s - C_LAG
            swap(r).wait_recv()
            s1[r] = (terms[c, r].astype(f32) + c_in[r].astype(f32)).astype(bf16)
            for i in range(ny - 1):
                along_y(i, r).start()

        @pl.when(s >= Y_LAG)
        def _():
            r = s - Y_LAG
            v = s1[r, y].astype(f32)
            for i in range(ny - 1):
                along_y(i, r).wait_recv()
                v = v + y_in[i, r].astype(f32)
            s2[r] = v.astype(bf16)

            @pl.when(2 * pair_at(r) + c != tile)
            def _():
                to_owner(r).start()

        @pl.when(s == P_STEP)
        def _():
            for i in range(nx - 1):
                parts_x(i).wait_recv()

            @pl.loop(0, nz)
            def _(k):
                v = parts[x * nz + k]
                for i in range(nx - 1):
                    v = v + px_in[i, k]
                psum[k] = v

            for i in range(nz - 1):
                parts_z(i).start()

    v = psum[z]
    for i in range(nz - 1):
        parts_z(i).wait_recv()
        v = v + pz_in[i]
    pooled[...] = v / pick(tile)

    finals = [(tile, (slide + d) % sz.slides) for d in range(1, sz.slides)]

    @pl.when(is_owner)
    def _():
        own[...] = s2[pairs - 1].astype(f32)

        @pl.loop(1, sz.tiles)
        def _(d):
            source = ((tile // 2) * 2 + sz.tiles - d) % sz.tiles
            source = source + (d // (sz.tiles - 1)) * ((tile // 2) * 2 + 1 - z % 2 - source)
            remote(s2.at[0], o_in.at[source], os.at[0], orr.at[source], mate).wait_recv()
            own[...] += o_in[source].astype(f32)

        final[...] = (own[...] / LOSS_SCALE).astype(bf16)
        for d, peer in enumerate(finals):
            remote(final, fin.at[y], fs.at[d], fr.at[y], peer).start()
        fin[y] = final[...]

    for q in range(ny):

        @pl.when(jnp.logical_not(is_owner & (y == q)))
        def _():
            remote(final, fin.at[q], fs.at[0], fr.at[q], finals[0]).wait_recv()

    every = [fin[q].astype(f32) for q in range(ny)]
    for tap in range(TAPS):
        rows = [v[tap * share : (tap + 1) * share] for v in every]
        block = jnp.concatenate(rows, axis=0).T
        result[tap] = jnp.concatenate([block[0:WIDTH], block[WIDTH:]], axis=1)

    @pl.when(is_owner)
    def _():
        for d, peer in enumerate(finals):
            remote(final, fin.at[y], fs.at[d], fr.at[y], peer).wait_send()

    for i in range(nz - 1):
        total_z(i).wait_send()
        rows_z(i, tile).wait_send()
        parts_z(i).wait_send()
    for i in range(nx - 1):
        total_x(i).wait_send()
        rows_x(i, x).wait_send()
        parts_x(i).wait_send()

    @pl.loop(0, pairs)
    def _(s):
        swap(s).wait_send()
        for i in range(ny - 1):
            along_y(i, s).wait_send()

        @pl.when(2 * pair_at(s) + c != tile)
        def _():
            to_owner(s).wait_send()


def shards(sz, tiles, counts, weights, slide_of, owner_map, cot, conv_weight):
    pairs, channels = sz.pairs, sz.tiles * WIDTH
    smem = pl.BlockSpec(memory_space=pltpu.SMEM)
    vmem = pl.BlockSpec(memory_space=pltpu.VMEM)
    hbm = pl.BlockSpec(memory_space=pltpu.MemorySpace.HBM)
    dma = pltpu.SemaphoreType.DMA
    pad = sz.packed_pad
    pooled, input_grad, weight_grad = pl.pallas_call(
        functools.partial(fused_kernel, sz),
        out_shape=(
            jax.ShapeDtypeStruct((pairs, LANES), f32),
            jax.ShapeDtypeStruct((SLOTS, SIDE, SIDE, 1, channels), f32),
            jax.ShapeDtypeStruct((TAPS, WIDTH, WIDTH), f32),
        ),
        in_specs=[smem] * 4 + [vmem] + [hbm] * 2,
        out_specs=(vmem, vmem, vmem),
        scratch_shapes=[
            pltpu.VMEM((pairs, SLOTS, SIDE, SIDE, LANES), bf16),
            pltpu.VMEM((pairs, TAPS, WIDTH, LANES), bf16),
            pltpu.VMEM((pairs, LANES), f32),
            pltpu.VMEM((sz.tiles, pairs, LANES), bf16),
            pltpu.VMEM((8, LANES), f32),
            pltpu.VMEM((sz.nz - 1, 8, LANES), f32),
            pltpu.VMEM((sz.nx - 1, 8, LANES), f32),
            pltpu.VMEM((8, LANES), f32),
            pltpu.VMEM((SLOTS, pairs, LANES), f32),
            pltpu.VMEM((PADDED, LANES), f32),
            pltpu.VMEM((PADDED, LANES), f32),
            pltpu.VMEM((pairs, ROWS, TAPS * LANES), bf16),
            pltpu.VMEM((ROWS, TAPS * LANES), bf16),
            pltpu.VMEM((TAPS * LANES, LANES), bf16),
            pltpu.VMEM((pairs, LANES, TAPS * LANES), bf16),
            pltpu.VMEM((pairs, ROWS, LANES), f32),
            pltpu.VMEM((sz.tiles, pairs, LANES), f32),
            pltpu.VMEM((2, pairs, sz.ny, pad, LANES), bf16),
            pltpu.VMEM((pairs, sz.ny, pad, LANES), bf16),
            pltpu.VMEM((pairs, sz.ny, pad, LANES), bf16),
            pltpu.VMEM((sz.ny - 1, pairs, pad, LANES), bf16),
            pltpu.VMEM((pairs, pad, LANES), bf16),
            pltpu.VMEM((sz.tiles, pad, LANES), bf16),
            pltpu.VMEM((pad, LANES), f32),
            pltpu.VMEM((pad, LANES), bf16),
            pltpu.VMEM((sz.ny, pad, LANES), bf16),
            pltpu.VMEM((sz.nx - 1, sz.nz, pairs, LANES), f32),
            pltpu.VMEM((sz.nz, pairs, LANES), f32),
            pltpu.VMEM((sz.nz - 1, pairs, LANES), f32),
        ]
        + [dma((pairs,))] * 2
        + [dma((sz.nz - 1,))] * 2
        + [dma((sz.nx - 1,))] * 2
        + [dma((sz.nz - 1,))] * 2
        + [dma((sz.nx - 1,))] * 2
        + [dma((pairs,))] * 2
        + [dma((sz.ny - 1, pairs))] * 2
        + [dma((pairs,)), dma((sz.tiles,))]
        + [dma((sz.slides,)), dma((sz.ny,))]
        + [dma((sz.nx - 1,))] * 2
        + [dma((sz.nz - 1,))] * 2,
        compiler_params=pltpu.CompilerParams(
            collective_id=0, has_side_effects=True, vmem_limit_bytes=56 * 1024 * 1024
        ),
        name="fused",
    )(counts, weights, slide_of[:, :, 0], owner_map, cot, tiles, conv_weight)
    input_grad = input_grad.reshape(1, SLOTS, SIDE, SIDE, channels)
    return pooled.reshape(1, 1, channels), input_grad, weight_grad


def solution(mesh):
    sz = Sizes(mesh)
    return jax.shard_map(
        functools.partial(shards, sz),
        mesh=mesh,
        in_specs=(
            P("slide", "tile", None, None, None),
            P("slide", "tile"),
            P("slide", "tile"),
            P("slide", "tile", None),
            P("slide", None),
            P("slide", "tile", None),
            P(),
        ),
        out_specs=(
            P("slide", "tile", None),
            P("slide", "tile", None, None, None),
            P(None, None, "tile"),
        ),
        check_vma=False,
    )
```

```python
import functools

import jax
import jax.numpy as jnp
from jax import lax
from jax.experimental import pallas as pl
from jax.experimental.pallas import tpu as pltpu
from jax.sharding import PartitionSpec as P

MESH = pl.DeviceIdType.MESH
LOSS_SCALE = 512.0
SIDE = 7
SLOTS = 3
WIDTH = 64
LANES = 128
TAPS = 9
ROWS = SLOTS * 64
BASE = 16
PADDED = BASE + ROWS + 16
f32 = jnp.float32
bf16 = jnp.bfloat16


class Sizes:
    def __init__(self, mesh):
        self.tiles = mesh.shape["tile"]
        self.slides = mesh.shape["slide"]
        self.ny = self.slides // 2
        self.nx = self.ny
        self.nz = self.tiles // self.nx
        self.pairs = self.tiles // 2
        self.share = 32 // self.ny
        self.packed = TAPS * self.share
        self.packed_pad = (self.packed + 15) // 16 * 16


def position(sz):
    tile = lax.axis_index("tile")
    slide = lax.axis_index("slide")
    return tile, slide, tile // sz.nz, tile % sz.nz, slide // 2, slide % 2


def remote(src, dst, send, recv, device):
    return pltpu.make_async_remote_copy(
        src_ref=src, dst_ref=dst, send_sem=send, recv_sem=recv, device_id=device, device_id_type=MESH
    )


def signal(device):
    pl.semaphore_signal(pltpu.get_barrier_semaphore(), inc=1, device_id=device, device_id_type=MESH)


def slot_route(slot, counts, weights, slide_of, owner_map):
    coef = jnp.where(slot < counts[0, 0], weights[0, slot], 0.0)
    return coef, owner_map[0, slide_of[0, slot]]


C_LAG = 4
Y_LAG = 9
X_LAG = 9
BARRIER_STEP = 1
Z_STEP = 6
P_STEP = 5


def fused_kernel(
    sz, counts, weights, slide_of, owner_map, cot, tiles_hbm, weight_hbm,
    pooled, input_grad, result,
    tiles, weight, stage, all_cot, my_total, z_total, x_total, total, grad,
    xp, gp, xc, gc, w_rows, w_lanes, slopes, parts, parts16,
    terms, c_in, s1, y_in, s2, x_in, s3, o_in, own, final, fin, px_in, psum, pz_in,
    tile_sem, weight_sem, gzs, gzr, gxs, gxr, tzs, tzr, txs, txr,
    cs, cr, ys, yr, os, orr, xs, xr, os3, fs, fr, pxs, pxr, pzs, pzr,
):
    tile, slide, x, z, y, c = position(sz)
    nx, ny, nz, pairs = sz.nx, sz.ny, sz.nz, sz.pairs
    share, nk = sz.share, nz // 2
    z_peers = [(x * nz + (z + off) % nz, slide) for off in range(1, nz)]
    x_peers = [(((x + off) % nx) * nz + z, slide) for off in range(1, nx)]
    mate = (tile, y * 2 + 1 - c)
    y_peers = [(tile, ((y + off) % ny) * 2 + c) for off in range(1, ny)]
    is_owner = (z % 2) == c

    def owner_k(s):
        return (z // 2 + 1 + s // nx) % nk

    def pair_at(s):
        return ((x + 1 + s % nx) % nx) * nk + owner_k(s)

    def lanes_of(s):
        return pl.ds(pl.multiple_of(pair_at(s) * LANES, LANES), LANES)

    def load(s):
        lanes = lanes_of(s)
        return (
            pltpu.make_async_copy(tiles_hbm.at[0, :, :, :, lanes], tiles.at[s], tile_sem.at[s]),
            pltpu.make_async_copy(weight_hbm.at[:, :, lanes], weight.at[s], weight_sem.at[s]),
        )

    @pl.loop(0, pairs)
    def _(s):
        for copy in load(s):
            copy.start()

    partners = z_peers + x_peers + y_peers + [mate]
    for peer in partners:
        signal(peer)

    xp[...] = jnp.zeros_like(xp)
    gp[...] = jnp.zeros_like(gp)
    for j in range(pairs):
        stage[pl.ds(j, 1), :] = cot[0, :, pl.ds(j * LANES, LANES)].astype(f32)
    all_cot[tile] = stage[...].astype(bf16)
    lane = lax.broadcasted_iota(jnp.int32, (8, LANES), 1)
    routes = [slot_route(s, counts, weights, slide_of, owner_map) for s in range(SLOTS)]
    mine = jnp.zeros((8, LANES), f32)
    for coef, target in routes:
        mine = mine + jnp.where(lane == target, coef, 0.0)
    my_total[...] = mine

    def total_z(i):
        return remote(my_total, z_total.at[i], tzs.at[i], tzr.at[i], z_peers[i])

    def rows_z(i, source):
        return remote(all_cot.at[source], all_cot.at[source], gzs.at[i], gzr.at[i], z_peers[i])

    def total_x(i):
        return remote(total, x_total.at[i], txs.at[i], txr.at[i], x_peers[i])

    def rows_x(i, source):
        block = all_cot.at[pl.ds(source * nz, nz)]
        return remote(block, block, gxs.at[i], gxr.at[i], x_peers[i])

    low64 = lax.broadcasted_iota(jnp.int32, (WIDTH, LANES), 1) < WIDTH
    row = lax.broadcasted_iota(jnp.int32, (64, LANES), 0)
    real = (row % 8 < SIDE) & (row < 8 * SIDE)
    owner_row = lax.broadcasted_iota(jnp.int32, (sz.tiles, LANES), 0)

    @pl.loop(0, pairs)
    def _(s):
        @pl.when(s == BARRIER_STEP)
        def _():
            pl.semaphore_wait(pltpu.get_barrier_semaphore(), len(partners))
            for i in range(nz - 1):
                total_z(i).start()
                rows_z(i, tile).start()

        @pl.when(s == min(Z_STEP, pairs - 1))
        def _():
            v = my_total[...]
            for i in range(nz - 1):
                total_z(i).wait_recv()
                rows_z(i, x * nz + (z + nz - 1 - i) % nz).wait_recv()
                v = v + z_total[i]
            total[...] = v
            for i in range(nx - 1):
                total_x(i).start()
                rows_x(i, x).start()

        for copy in load(s):
            copy.wait()
        for tap in range(TAPS):
            w = weight[s, tap]
            zero = jnp.zeros_like(w)
            first, second = jnp.where(low64, w, zero), jnp.where(low64, zero, w)
            w_rows[pl.ds(tap * LANES, WIDTH), :] = first
            w_rows[pl.ds(tap * LANES + WIDTH, WIDTH), :] = second
            w_lanes[s, pl.ds(0, WIDTH), pl.ds(tap * LANES, LANES)] = first
            w_lanes[s, pl.ds(WIDTH, WIDTH), pl.ds(tap * LANES, LANES)] = second
        for t in range(SLOTS):
            for h in range(SIDE):
                xp[pl.ds(BASE + 64 * t + 8 * h, SIDE), :] = tiles[s, t, h].astype(f32)
        for tap in range(TAPS):
            shift = 8 * (tap // 3 - 1) + tap % 3 - 1
            xc[s, :, pl.ds(tap * LANES, LANES)] = xp[pl.ds(BASE + shift, ROWS), :].astype(bf16)
        pre = jnp.dot(xc[s], w_rows[...], preferred_element_type=f32)
        sigma = 1.0 / (1.0 + jnp.exp(-pre))
        part = jnp.zeros((sz.tiles, LANES), f32)
        for t in range(SLOTS):
            v, q = pre[64 * t : 64 * t + 64], sigma[64 * t : 64 * t + 64]
            mean = jnp.sum(jnp.where(real, v * q, 0.0), axis=0, keepdims=True) / (SIDE * SIDE)
            embedding = mean.astype(bf16).astype(f32)
            coef, target = routes[t]
            part = part + jnp.where(owner_row == target, coef, 0.0) * embedding
            slope = q * (1.0 + v * (1.0 - q))
            slopes[s, pl.ds(64 * t, 64), :] = jnp.where(real, slope, 0.0)
        parts[:, pl.ds(pair_at(s), 1), :] = part.reshape(sz.tiles, 1, LANES)

    def parts_x(i):
        xo = (x + i + 1) % nx
        return remote(parts16.at[pl.ds(xo * nz, nz)], px_in.at[i], pxs.at[i], pxr.at[i], x_peers[i])

    def parts_z(i):
        return remote(psum.at[(z + i + 1) % nz], pz_in.at[i], pzs.at[i], pzr.at[i], z_peers[i])

    parts16[...] = parts[...].astype(bf16)
    for i in range(nx - 1):
        parts_x(i).start()
    v = total[...]
    for i in range(nx - 1):
        total_x(i).wait_recv()
        rows_x(i, (x + nx - 1 - i) % nx).wait_recv()
        v = v + x_total[i]
    denominator = jnp.maximum(v, 1.0)

    def pick(owner):
        found = jnp.sum(jnp.where(lane == owner, denominator, 0.0), axis=1, keepdims=True)
        return jnp.broadcast_to(found[0:1], (pairs, LANES))

    for t, (coef, target) in enumerate(routes):
        scaled = (LOSS_SCALE * all_cot[target].astype(f32) / pick(target)).astype(bf16)
        grad[t] = coef * scaled.astype(f32)

    def swap(s):
        return remote(terms.at[1 - c, s], c_in.at[s], cs.at[s], cr.at[s], mate)

    def along_y(i, s):
        return remote(s1.at[s, (y + i + 1) % ny], y_in.at[i, s], ys.at[i, s], yr.at[i, s], y_peers[i])

    def to_owner(s):
        device = (2 * pair_at(s) + c, slide)
        return remote(s2.at[s], o_in.at[z, x], os.at[s], orr.at[z, x], device)

    def along_x(s):
        device = (((x + 1 + s % nx) % nx) * nz + z, slide)
        m, i = s // (2 * nx), s % nx
        return remote(s1.at[s], x_in.at[m, i], xs.at[m, i], xr.at[m, i], device)

    def to_owner_y(s, q):
        device = (x * nz + 2 * owner_k(s) + c, q * 2 + c)
        m = s // (2 * nx)
        return remote(s3.at[m, q], o_in.at[z, y], os3.at[m, q], orr.at[z, y], device)

    def by_y(s):
        return (s // nx) % 2 == 0

    def mine_at(s, q):
        return is_owner & (owner_k(s) == z // 2) & (q == y)

    low = lax.broadcasted_iota(jnp.int32, (32, LANES), 1) < WIDTH
    none = jnp.zeros((share, LANES), f32)

    def pre_grad(s):
        upstream = [grad[t, pl.ds(pair_at(s), 1), :] / (SIDE * SIDE) for t in range(SLOTS)]
        return [upstream[t] * slopes[s, pl.ds(64 * t, 64), :] for t in range(SLOTS)]

    @pl.loop(0, pairs + Y_LAG)
    def _(s):
        @pl.when(s < pairs)
        def _():
            g = jnp.concatenate(pre_grad(s), axis=0).astype(bf16)
            dw = jnp.dot(g.T, xc[s], preferred_element_type=f32)
            even, odd = [], []
            for tap in range(TAPS):
                d = dw[:, tap * LANES : (tap + 1) * LANES]
                even.append(jnp.where(low, d[0:32], pltpu.roll(d[32:64], WIDTH, 1)))
                odd.append(jnp.where(low, pltpu.roll(d[64:96], WIDTH, 1), d[96:128]))
            per = 16 // share
            for parity, rows in enumerate((even, odd)):
                for yy in range(ny):
                    for j in range(sz.packed_pad // 16):
                        block = [
                            rows[tap][yy * share : (yy + 1) * share] if tap < TAPS else none
                            for tap in range(j * per, (j + 1) * per)
                        ]
                        terms[parity, s, yy, pl.ds(16 * j, 16), :] = jnp.concatenate(block, axis=0).astype(bf16)
            swap(s).start()

        @pl.when((s >= X_LAG) & (s < pairs + X_LAG))
        def _():
            r = s - X_LAG
            for t, rows in enumerate(pre_grad(r)):
                gp[pl.ds(BASE + 64 * t, 64), :] = rows
            for tap in range(TAPS):
                shift = 8 * (tap // 3 - 1) + tap % 3 - 1
                gc[:, pl.ds(tap * LANES, LANES)] = gp[pl.ds(BASE - shift, ROWS), :].astype(bf16)
            dx = lax.dot_general(
                gc[...], w_lanes[r], (((1,), (1,)), ((), ())), preferred_element_type=f32
            )
            lanes = lanes_of(r)
            for t in range(SLOTS):
                for h in range(SIDE):
                    at = 64 * t + 8 * h
                    input_grad[t, h, :, :, lanes] = dx[at : at + SIDE].reshape(SIDE, 1, LANES)

        @pl.when((s >= C_LAG) & (s < pairs + C_LAG))
        def _():
            r = s - C_LAG
            swap(r).wait_recv()
            s1[r] = (terms[c, r].astype(f32) + c_in[r].astype(f32)).astype(bf16)

            @pl.when(by_y(r))
            def _():
                for i in range(ny - 1):
                    along_y(i, r).start()

            @pl.when(jnp.logical_not(by_y(r)) & (r % nx != nx - 1))
            def _():
                along_x(r).start()

        @pl.when((s >= Y_LAG) & by_y(s - Y_LAG))
        def _():
            r = s - Y_LAG
            v = s1[r, y].astype(f32)
            for i in range(ny - 1):
                along_y(i, r).wait_recv()
                v = v + y_in[i, r].astype(f32)
            s2[r] = v.astype(bf16)
            to_owner(r).start()

        @pl.when((s >= Y_LAG) & jnp.logical_not(by_y(s - Y_LAG)) & ((s - Y_LAG) % nx == nx - 1))
        def _():
            r = s - Y_LAG
            m = r // (2 * nx)
            v = s1[r].astype(f32)
            for i in range(nx - 1):
                along_x(r - nx + 1 + i).wait_recv()
                v = v + x_in[m, i].astype(f32)
            s3[m] = v.astype(bf16)
            for q in range(ny):

                @pl.when(jnp.logical_not(mine_at(r, q)))
                def _():
                    to_owner_y(r, q).start()

        @pl.when(s == P_STEP)
        def _():
            for i in range(nx - 1):
                parts_x(i).wait_recv()

            @pl.loop(0, nz)
            def _(k):
                v = parts[x * nz + k]
                for i in range(nx - 1):
                    v = v + px_in[i, k].astype(f32)
                psum[k] = v.astype(bf16)

            for i in range(nz - 1):
                parts_z(i).start()

    v = psum[z].astype(f32)
    for i in range(nz - 1):
        parts_z(i).wait_recv()
        v = v + pz_in[i].astype(f32)
    pooled[...] = v / pick(tile)

    finals = [(tile, (slide + d) % sz.slides) for d in range(1, sz.slides)]

    @pl.when(is_owner)
    def _():
        own[...] = s3[nk // 2 - 1, y].astype(f32)

        @pl.loop(0, sz.nz * nx)
        def _(d):
            from_z = 2 * ((z // 2 + nk - 1 - d // (2 * nx)) % nk) + (d // nx) % 2
            i = d % nx

            @pl.when(jnp.logical_not((from_z == z) & (i == y)))
            def _():
                remote(s2.at[0], o_in.at[from_z, i], os.at[0], orr.at[from_z, i], mate).wait_recv()
                own[...] += o_in[from_z, i].astype(f32)

        final[...] = (own[...] / LOSS_SCALE).astype(bf16)
        for d, peer in enumerate(finals):
            remote(final, fin.at[y], fs.at[d], fr.at[y], peer).start()
        fin[y] = final[...]

    for q in range(ny):

        @pl.when(jnp.logical_not(is_owner & (y == q)))
        def _():
            remote(final, fin.at[q], fs.at[0], fr.at[q], finals[0]).wait_recv()

    every = [fin[q].astype(f32) for q in range(ny)]
    for tap in range(TAPS):
        rows = [v[tap * share : (tap + 1) * share] for v in every]
        block = jnp.concatenate(rows, axis=0).T
        result[tap] = jnp.concatenate([block[0:WIDTH], block[WIDTH:]], axis=1)

    @pl.when(is_owner)
    def _():
        for d, peer in enumerate(finals):
            remote(final, fin.at[y], fs.at[d], fr.at[y], peer).wait_send()

    for i in range(nz - 1):
        total_z(i).wait_send()
        rows_z(i, tile).wait_send()
        parts_z(i).wait_send()
    for i in range(nx - 1):
        total_x(i).wait_send()
        rows_x(i, x).wait_send()
        parts_x(i).wait_send()

    @pl.loop(0, pairs)
    def _(s):
        swap(s).wait_send()

        @pl.when(by_y(s))
        def _():
            for i in range(ny - 1):
                along_y(i, s).wait_send()
            to_owner(s).wait_send()

        @pl.when(jnp.logical_not(by_y(s)) & (s % nx != nx - 1))
        def _():
            along_x(s).wait_send()

        @pl.when(jnp.logical_not(by_y(s)) & (s % nx == nx - 1))
        def _():
            for q in range(ny):

                @pl.when(jnp.logical_not(mine_at(s, q)))
                def _():
                    to_owner_y(s, q).wait_send()


def shards(sz, tiles, counts, weights, slide_of, owner_map, cot, conv_weight):
    pairs, channels = sz.pairs, sz.tiles * WIDTH
    smem = pl.BlockSpec(memory_space=pltpu.SMEM)
    vmem = pl.BlockSpec(memory_space=pltpu.VMEM)
    hbm = pl.BlockSpec(memory_space=pltpu.MemorySpace.HBM)
    dma = pltpu.SemaphoreType.DMA
    pad = sz.packed_pad
    pooled, input_grad, weight_grad = pl.pallas_call(
        functools.partial(fused_kernel, sz),
        out_shape=(
            jax.ShapeDtypeStruct((pairs, LANES), f32),
            jax.ShapeDtypeStruct((SLOTS, SIDE, SIDE, 1, channels), f32),
            jax.ShapeDtypeStruct((TAPS, WIDTH, WIDTH), f32),
        ),
        in_specs=[smem] * 4 + [vmem] + [hbm] * 2,
        out_specs=(vmem, vmem, vmem),
        scratch_shapes=[
            pltpu.VMEM((pairs, SLOTS, SIDE, SIDE, LANES), bf16),
            pltpu.VMEM((pairs, TAPS, WIDTH, LANES), bf16),
            pltpu.VMEM((pairs, LANES), f32),
            pltpu.VMEM((sz.tiles, pairs, LANES), bf16),
            pltpu.VMEM((8, LANES), f32),
            pltpu.VMEM((sz.nz - 1, 8, LANES), f32),
            pltpu.VMEM((sz.nx - 1, 8, LANES), f32),
            pltpu.VMEM((8, LANES), f32),
            pltpu.VMEM((SLOTS, pairs, LANES), f32),
            pltpu.VMEM((PADDED, LANES), f32),
            pltpu.VMEM((PADDED, LANES), f32),
            pltpu.VMEM((pairs, ROWS, TAPS * LANES), bf16),
            pltpu.VMEM((ROWS, TAPS * LANES), bf16),
            pltpu.VMEM((TAPS * LANES, LANES), bf16),
            pltpu.VMEM((pairs, LANES, TAPS * LANES), bf16),
            pltpu.VMEM((pairs, ROWS, LANES), f32),
            pltpu.VMEM((sz.tiles, pairs, LANES), f32),
            pltpu.VMEM((sz.tiles, pairs, LANES), bf16),
            pltpu.VMEM((2, pairs, sz.ny, pad, LANES), bf16),
            pltpu.VMEM((pairs, sz.ny, pad, LANES), bf16),
            pltpu.VMEM((pairs, sz.ny, pad, LANES), bf16),
            pltpu.VMEM((sz.ny - 1, pairs, pad, LANES), bf16),
            pltpu.VMEM((pairs, pad, LANES), bf16),
            pltpu.VMEM((sz.nz // 4, sz.nx - 1, sz.ny, pad, LANES), bf16),
            pltpu.VMEM((sz.nz // 4, sz.ny, pad, LANES), bf16),
            pltpu.VMEM((sz.nz, sz.nx, pad, LANES), bf16),
            pltpu.VMEM((pad, LANES), f32),
            pltpu.VMEM((pad, LANES), bf16),
            pltpu.VMEM((sz.ny, pad, LANES), bf16),
            pltpu.VMEM((sz.nx - 1, sz.nz, pairs, LANES), bf16),
            pltpu.VMEM((sz.nz, pairs, LANES), bf16),
            pltpu.VMEM((sz.nz - 1, pairs, LANES), bf16),
        ]
        + [dma((pairs,))] * 2
        + [dma((sz.nz - 1,))] * 2
        + [dma((sz.nx - 1,))] * 2
        + [dma((sz.nz - 1,))] * 2
        + [dma((sz.nx - 1,))] * 2
        + [dma((pairs,))] * 2
        + [dma((sz.ny - 1, pairs))] * 2
        + [dma((pairs,)), dma((sz.nz, sz.nx))]
        + [dma((sz.nz // 4, sz.nx - 1))] * 2
        + [dma((sz.nz // 4, sz.ny))]
        + [dma((sz.slides,)), dma((sz.ny,))]
        + [dma((sz.nx - 1,))] * 2
        + [dma((sz.nz - 1,))] * 2,
        compiler_params=pltpu.CompilerParams(
            collective_id=0, has_side_effects=True, vmem_limit_bytes=56 * 1024 * 1024
        ),
        name="fused",
    )(counts, weights, slide_of[:, :, 0], owner_map, cot, tiles, conv_weight)
    input_grad = input_grad.reshape(1, SLOTS, SIDE, SIDE, channels)
    return pooled.reshape(1, 1, channels), input_grad, weight_grad


def solution(mesh):
    sz = Sizes(mesh)
    return jax.shard_map(
        functools.partial(shards, sz),
        mesh=mesh,
        in_specs=(
            P("slide", "tile", None, None, None),
            P("slide", "tile"),
            P("slide", "tile"),
            P("slide", "tile", None),
            P("slide", None),
            P("slide", "tile", None),
            P(),
        ),
        out_specs=(
            P("slide", "tile", None),
            P("slide", "tile", None, None, None),
            P(None, None, "tile"),
        ),
        check_vma=False,
    )
```

```python
import functools

import jax
import jax.numpy as jnp
from jax import lax
from jax.experimental import pallas as pl
from jax.experimental.pallas import tpu as pltpu
from jax.sharding import PartitionSpec as P

MESH = pl.DeviceIdType.MESH
LOSS_SCALE = 512.0
SIDE = 7
SLOTS = 3
WIDTH = 64
LANES = 128
TAPS = 9
ROWS = SLOTS * 64
BASE = 16
PADDED = BASE + ROWS + 16
f32 = jnp.float32
bf16 = jnp.bfloat16


class Sizes:
    def __init__(self, mesh):
        self.tiles = mesh.shape["tile"]
        self.slides = mesh.shape["slide"]
        self.ny = self.slides // 2
        self.nx = self.ny
        self.nz = self.tiles // self.nx
        self.pairs = self.tiles // 2
        self.share = 32 // self.ny
        self.packed = TAPS * self.share
        self.packed_pad = (self.packed + 15) // 16 * 16


def position(sz):
    tile = lax.axis_index("tile")
    slide = lax.axis_index("slide")
    return tile, slide, tile // sz.nz, tile % sz.nz, slide // 2, slide % 2


def remote(src, dst, send, recv, device):
    return pltpu.make_async_remote_copy(
        src_ref=src, dst_ref=dst, send_sem=send, recv_sem=recv, device_id=device, device_id_type=MESH
    )


def signal(device):
    pl.semaphore_signal(pltpu.get_barrier_semaphore(), inc=1, device_id=device, device_id_type=MESH)


def slot_route(slot, counts, weights, slide_of, owner_map):
    coef = jnp.where(slot < counts[0, 0], weights[0, slot], 0.0)
    return coef, owner_map[0, slide_of[0, slot]]


C_LAG = 3
Y_LAG = 12
X_LAG = 3
X_COUNT = 0
X_MIDDLE = 12
BARRIER_STEP = 0
Z_STEP = 6
P_STEP = 17


def fused_kernel(
    sz, counts, weights, slide_of, owner_map, cot, tiles_hbm, weight_hbm,
    pooled, input_grad, result,
    tiles, weight, stage, all_cot, my_total, z_total, x_total, total, grad,
    xp, gp, xc, gc, w_rows, w_lanes, slopes, parts, parts16,
    terms, c_in, s1, y_in, s2, x_in, s3, o_in, own, final, fin, px_in, psum, pz_in,
    tile_sem, weight_sem, gzs, gzr, gxs, gxr, tzs, tzr, txs, txr,
    cs, cr, ys, yr, os, orr, xs, xr, os3, fs, fr, ms, mr, pxs, pxr, pzs, pzr,
):
    tile, slide, x, z, y, c = position(sz)
    nx, ny, nz, pairs = sz.nx, sz.ny, sz.nz, sz.pairs
    share, nk = sz.share, nz // 2
    early, middle = min(X_COUNT, pairs), min(X_MIDDLE, pairs)
    z_peers = [(x * nz + (z + off) % nz, slide) for off in range(1, nz)]
    x_peers = [(((x + off) % nx) * nz + z, slide) for off in range(1, nx)]
    mate = (tile, y * 2 + 1 - c)
    y_peers = [(tile, ((y + off) % ny) * 2 + c) for off in range(1, ny)]
    is_owner = (z % 2) == c

    def owner_k(s):
        return (z // 2 + 1 + s // nx) % nk

    def pair_at(s):
        return ((x + 1 + s % nx) % nx) * nk + owner_k(s)

    def lanes_of(s):
        return pl.ds(pl.multiple_of(pair_at(s) * LANES, LANES), LANES)

    def load(s):
        lanes = lanes_of(s)
        return (
            pltpu.make_async_copy(tiles_hbm.at[0, :, :, :, lanes], tiles.at[s], tile_sem.at[s]),
            pltpu.make_async_copy(weight_hbm.at[:, :, lanes], weight.at[s], weight_sem.at[s]),
        )

    partners = z_peers + x_peers + y_peers + [mate]
    for peer in partners:
        signal(peer)

    for j in range(pairs):
        stage[pl.ds(j, 1), :] = cot[0, :, pl.ds(j * LANES, LANES)].astype(f32)
    all_cot[tile] = stage[...].astype(bf16)
    lane = lax.broadcasted_iota(jnp.int32, (8, LANES), 1)
    routes = [slot_route(s, counts, weights, slide_of, owner_map) for s in range(SLOTS)]
    mine = jnp.zeros((8, LANES), f32)
    for coef, target in routes:
        mine = mine + jnp.where(lane == target, coef, 0.0)
    my_total[...] = mine

    @pl.loop(0, pairs)
    def _(s):
        for copy in load(s):
            copy.start()

    xp[...] = jnp.zeros_like(xp)
    gp[...] = jnp.zeros_like(gp)

    def total_z(i):
        return remote(my_total, z_total.at[i], tzs.at[i], tzr.at[i], z_peers[i])

    def rows_z(i, source):
        return remote(all_cot.at[source], all_cot.at[source], gzs.at[i], gzr.at[i], z_peers[i])

    def total_x(i):
        return remote(total, x_total.at[i], txs.at[i], txr.at[i], x_peers[i])

    def rows_x(i, source):
        block = all_cot.at[pl.ds(source * nz, nz)]
        return remote(block, block, gxs.at[i], gxr.at[i], x_peers[i])

    low64 = lax.broadcasted_iota(jnp.int32, (WIDTH, LANES), 1) < WIDTH
    row = lax.broadcasted_iota(jnp.int32, (64, LANES), 0)
    real = (row % 8 < SIDE) & (row < 8 * SIDE)
    owner_row = lax.broadcasted_iota(jnp.int32, (sz.tiles, LANES), 0)

    @pl.loop(0, pairs)
    def _(s):
        @pl.when(s == BARRIER_STEP)
        def _():
            pl.semaphore_wait(pltpu.get_barrier_semaphore(), len(partners))
            for i in range(nz - 1):
                total_z(i).start()
                rows_z(i, tile).start()

        @pl.when(s == min(Z_STEP, pairs - 1))
        def _():
            v = my_total[...]
            for i in range(nz - 1):
                total_z(i).wait_recv()
                rows_z(i, x * nz + (z + nz - 1 - i) % nz).wait_recv()
                v = v + z_total[i]
            total[...] = v
            for i in range(nx - 1):
                total_x(i).start()
                rows_x(i, x).start()

        for copy in load(s):
            copy.wait()
        for tap in range(TAPS):
            w = weight[s, tap]
            zero = jnp.zeros_like(w)
            first, second = jnp.where(low64, w, zero), jnp.where(low64, zero, w)
            w_rows[pl.ds(tap * LANES, WIDTH), :] = first
            w_rows[pl.ds(tap * LANES + WIDTH, WIDTH), :] = second
            w_lanes[s, pl.ds(0, WIDTH), pl.ds(tap * LANES, LANES)] = first
            w_lanes[s, pl.ds(WIDTH, WIDTH), pl.ds(tap * LANES, LANES)] = second
        for t in range(SLOTS):
            for h in range(SIDE):
                xp[pl.ds(BASE + 64 * t + 8 * h, SIDE), :] = tiles[s, t, h].astype(f32)
        for tap in range(TAPS):
            shift = 8 * (tap // 3 - 1) + tap % 3 - 1
            xc[s, :, pl.ds(tap * LANES, LANES)] = xp[pl.ds(BASE + shift, ROWS), :].astype(bf16)
        pre = jnp.dot(xc[s], w_rows[...], preferred_element_type=f32)
        sigma = 1.0 / (1.0 + jnp.exp(-pre))
        part = jnp.zeros((sz.tiles, LANES), f32)
        for t in range(SLOTS):
            v, q = pre[64 * t : 64 * t + 64], sigma[64 * t : 64 * t + 64]
            mean = jnp.sum(jnp.where(real, v * q, 0.0), axis=0, keepdims=True) / (SIDE * SIDE)
            embedding = mean.astype(bf16).astype(f32)
            coef, target = routes[t]
            part = part + jnp.where(owner_row == target, coef, 0.0) * embedding
            slope = q * (1.0 + v * (1.0 - q))
            slopes[s, pl.ds(64 * t, 64), :] = jnp.where(real, slope, 0.0)
        parts[:, pl.ds(pair_at(s), 1), :] = part.reshape(sz.tiles, 1, LANES)

    def parts_x(i):
        xo = (x + i + 1) % nx
        return remote(parts16.at[pl.ds(xo * nz, nz)], px_in.at[i], pxs.at[i], pxr.at[i], x_peers[i])

    def parts_z(i):
        return remote(psum.at[(z + i + 1) % nz], pz_in.at[i], pzs.at[i], pzr.at[i], z_peers[i])

    parts16[...] = parts[...].astype(bf16)
    for i in range(nx - 1):
        parts_x(i).start()
    v = total[...]
    for i in range(nx - 1):
        total_x(i).wait_recv()
        rows_x(i, (x + nx - 1 - i) % nx).wait_recv()
        v = v + x_total[i]
    denominator = jnp.maximum(v, 1.0)

    def pick(owner):
        found = jnp.sum(jnp.where(lane == owner, denominator, 0.0), axis=1, keepdims=True)
        return jnp.broadcast_to(found[0:1], (pairs, LANES))

    for t, (coef, target) in enumerate(routes):
        scaled = (LOSS_SCALE * all_cot[target].astype(f32) / pick(target)).astype(bf16)
        grad[t] = coef * scaled.astype(f32)

    def swap(s):
        return remote(terms.at[1 - c, s], c_in.at[s], cs.at[s], cr.at[s], mate)

    def along_y(i, s):
        return remote(s1.at[s, (y + i + 1) % ny], y_in.at[i, s], ys.at[i, s], yr.at[i, s], y_peers[i])

    def to_owner(s):
        device = (2 * pair_at(s) + c, slide)
        return remote(s2.at[s], o_in.at[z, x], os.at[s], orr.at[z, x], device)

    def along_x(s):
        device = (((x + 1 + s % nx) % nx) * nz + z, slide)
        m, i = s // (2 * nx), s % nx
        return remote(s1.at[s], x_in.at[m, i], xs.at[m, i], xr.at[m, i], device)

    def to_owner_y(s, q):
        device = (x * nz + 2 * owner_k(s) + c, q * 2 + c)
        m = s // (2 * nx)
        return remote(s3.at[m, q], o_in.at[z, y], os3.at[m, q], orr.at[z, y], device)

    def by_y(s):
        return (s // nx) % 2 == 0

    def mine_at(s, q):
        return is_owner & (owner_k(s) == z // 2) & (q == y)

    low = lax.broadcasted_iota(jnp.int32, (32, LANES), 1) < WIDTH
    none = jnp.zeros((share, LANES), f32)

    def pre_grad(s):
        upstream = [grad[t, pl.ds(pair_at(s), 1), :] / (SIDE * SIDE) for t in range(SLOTS)]
        return [upstream[t] * slopes[s, pl.ds(64 * t, 64), :] for t in range(SLOTS)]

    def input_gradient(r):
        for t, rows in enumerate(pre_grad(r)):
            gp[pl.ds(BASE + 64 * t, 64), :] = rows
        for tap in range(TAPS):
            shift = 8 * (tap // 3 - 1) + tap % 3 - 1
            gc[:, pl.ds(tap * LANES, LANES)] = gp[pl.ds(BASE - shift, ROWS), :].astype(bf16)
        dx = lax.dot_general(
            gc[...], w_lanes[r], (((1,), (1,)), ((), ())), preferred_element_type=f32
        )
        lanes = lanes_of(r)
        for t in range(SLOTS):
            for h in range(SIDE):
                at = 64 * t + 8 * h
                input_grad[t, h, :, :, lanes] = dx[at : at + SIDE].reshape(SIDE, 1, LANES)

    @pl.loop(0, pairs + Y_LAG)
    def _(s):
        @pl.when(s < pairs)
        def _():
            g = jnp.concatenate(pre_grad(s), axis=0).astype(bf16)
            dw = jnp.dot(g.T, xc[s], preferred_element_type=f32)
            even, odd = [], []
            for tap in range(TAPS):
                d = dw[:, tap * LANES : (tap + 1) * LANES]
                even.append(jnp.where(low, d[0:32], pltpu.roll(d[32:64], WIDTH, 1)))
                odd.append(jnp.where(low, pltpu.roll(d[64:96], WIDTH, 1), d[96:128]))
            per = 16 // share
            for parity, rows in enumerate((even, odd)):
                for yy in range(ny):
                    for j in range(sz.packed_pad // 16):
                        block = [
                            rows[tap][yy * share : (yy + 1) * share] if tap < TAPS else none
                            for tap in range(j * per, (j + 1) * per)
                        ]
                        terms[parity, s, yy, pl.ds(16 * j, 16), :] = jnp.concatenate(block, axis=0).astype(bf16)
            swap(s).start()

        @pl.when((s >= X_LAG) & (s < early + X_LAG))
        def _():
            input_gradient(s - X_LAG)

        @pl.when((s >= C_LAG) & (s < pairs + C_LAG))
        def _():
            r = s - C_LAG
            swap(r).wait_recv()
            s1[r] = (terms[c, r].astype(f32) + c_in[r].astype(f32)).astype(bf16)

            @pl.when(by_y(r))
            def _():
                for i in range(ny - 1):
                    along_y(i, r).start()

            @pl.when(jnp.logical_not(by_y(r)) & (r % nx != nx - 1))
            def _():
                along_x(r).start()

        @pl.when((s >= Y_LAG) & by_y(s - Y_LAG))
        def _():
            r = s - Y_LAG
            v = s1[r, y].astype(f32)
            for i in range(ny - 1):
                along_y(i, r).wait_recv()
                v = v + y_in[i, r].astype(f32)
            s2[r] = v.astype(bf16)
            to_owner(r).start()

        @pl.when((s >= Y_LAG) & jnp.logical_not(by_y(s - Y_LAG)) & ((s - Y_LAG) % nx == nx - 1))
        def _():
            r = s - Y_LAG
            m = r // (2 * nx)
            v = s1[r].astype(f32)
            for i in range(nx - 1):
                along_x(r - nx + 1 + i).wait_recv()
                v = v + x_in[m, i].astype(f32)
            s3[m] = v.astype(bf16)
            for q in range(ny):

                @pl.when(jnp.logical_not(mine_at(r, q)))
                def _():
                    to_owner_y(r, q).start()

        @pl.when(s == min(P_STEP, pairs + Y_LAG - 1))
        def _():
            for i in range(nx - 1):
                parts_x(i).wait_recv()

            @pl.loop(0, nz)
            def _(k):
                v = parts[x * nz + k]
                for i in range(nx - 1):
                    v = v + px_in[i, k].astype(f32)
                psum[k] = v.astype(bf16)

            for i in range(nz - 1):
                parts_z(i).start()

    @pl.loop(early, middle)
    def _(s):
        input_gradient(s)

    v = psum[z].astype(f32)
    for i in range(nz - 1):
        parts_z(i).wait_recv()
        v = v + pz_in[i].astype(f32)
    pooled[...] = v / pick(tile)

    def final_y(i):
        return remote(final, fin.at[y], fs.at[i], fr.at[i], y_peers[i])

    def final_mate(i):
        piece = fin.at[(y + ny - i) % ny]
        return remote(piece, piece, ms.at[i], mr.at[i], mate)

    @pl.when(is_owner)
    def _():
        own[...] = s3[nk // 2 - 1, y].astype(f32)

        @pl.loop(0, sz.nz * nx)
        def _(d):
            from_z = 2 * ((z // 2 + nk - 1 - d // (2 * nx)) % nk) + (d // nx) % 2
            i = d % nx

            @pl.when(jnp.logical_not((from_z == z) & (i == y)))
            def _():
                remote(s2.at[0], o_in.at[from_z, i], os.at[0], orr.at[from_z, i], mate).wait_recv()
                own[...] += o_in[from_z, i].astype(f32)

        final[...] = (own[...] / LOSS_SCALE).astype(bf16)
        for i in range(ny - 1):
            final_y(i).start()
        fin[y] = final[...]
        final_mate(0).start()

    @pl.loop(middle, pairs)
    def _(s):
        input_gradient(s)

    for i in range(nz - 1):
        total_z(i).wait_send()
        rows_z(i, tile).wait_send()
        parts_z(i).wait_send()
    for i in range(nx - 1):
        total_x(i).wait_send()
        rows_x(i, x).wait_send()
        parts_x(i).wait_send()

    @pl.loop(0, pairs)
    def _(s):
        swap(s).wait_send()

        @pl.when(by_y(s))
        def _():
            for i in range(ny - 1):
                along_y(i, s).wait_send()
            to_owner(s).wait_send()

        @pl.when(jnp.logical_not(by_y(s)) & (s % nx != nx - 1))
        def _():
            along_x(s).wait_send()

        @pl.when(jnp.logical_not(by_y(s)) & (s % nx == nx - 1))
        def _():
            for q in range(ny):

                @pl.when(jnp.logical_not(mine_at(s, q)))
                def _():
                    to_owner_y(s, q).wait_send()

    @pl.when(is_owner)
    def _():
        for i in range(ny - 1):
            piece = fin.at[(y + ny - 1 - i) % ny]
            remote(final, piece, fs.at[i], fr.at[i], y_peers[i]).wait_recv()
            final_mate(i + 1).start()

    @pl.when(jnp.logical_not(is_owner))
    def _():
        for i in range(ny):
            final_mate(i).wait_recv()

    every = [fin[q].astype(f32) for q in range(ny)]
    for tap in range(TAPS):
        rows = [v[tap * share : (tap + 1) * share] for v in every]
        block = jnp.concatenate(rows, axis=0).T
        result[tap] = jnp.concatenate([block[0:WIDTH], block[WIDTH:]], axis=1)

    @pl.when(is_owner)
    def _():
        for i in range(ny - 1):
            final_y(i).wait_send()
        for i in range(ny):
            final_mate(i).wait_send()


def finish_kernel(a, b, c, a_out, b_out, c_out, sems):
    copies = [
        pltpu.make_async_copy(src, dst, sems.at[i])
        for i, (src, dst) in enumerate(((a, a_out), (b, b_out), (c, c_out)))
    ]
    for copy in copies:
        copy.start()
    for copy in copies:
        copy.wait()


def shards(sz, tiles, counts, weights, slide_of, owner_map, cot, conv_weight):
    pairs, channels = sz.pairs, sz.tiles * WIDTH
    smem = pl.BlockSpec(memory_space=pltpu.SMEM)
    vmem = pl.BlockSpec(memory_space=pltpu.VMEM)
    hbm = pl.BlockSpec(memory_space=pltpu.MemorySpace.HBM)
    dma = pltpu.SemaphoreType.DMA
    pad = sz.packed_pad
    results = (
        jax.ShapeDtypeStruct((pairs, LANES), f32),
        jax.ShapeDtypeStruct((SLOTS, SIDE, SIDE, 1, channels), f32),
        jax.ShapeDtypeStruct((TAPS, WIDTH, WIDTH), f32),
    )
    made = pl.pallas_call(
        functools.partial(fused_kernel, sz),
        out_shape=tuple(pltpu.VMEM(r.shape, r.dtype) for r in results),
        in_specs=[smem] * 4 + [vmem] + [hbm] * 2,
        out_specs=(vmem, vmem, vmem),
        scratch_shapes=[
            pltpu.VMEM((pairs, SLOTS, SIDE, SIDE, LANES), bf16),
            pltpu.VMEM((pairs, TAPS, WIDTH, LANES), bf16),
            pltpu.VMEM((pairs, LANES), f32),
            pltpu.VMEM((sz.tiles, pairs, LANES), bf16),
            pltpu.VMEM((8, LANES), f32),
            pltpu.VMEM((sz.nz - 1, 8, LANES), f32),
            pltpu.VMEM((sz.nx - 1, 8, LANES), f32),
            pltpu.VMEM((8, LANES), f32),
            pltpu.VMEM((SLOTS, pairs, LANES), f32),
            pltpu.VMEM((PADDED, LANES), f32),
            pltpu.VMEM((PADDED, LANES), f32),
            pltpu.VMEM((pairs, ROWS, TAPS * LANES), bf16),
            pltpu.VMEM((ROWS, TAPS * LANES), bf16),
            pltpu.VMEM((TAPS * LANES, LANES), bf16),
            pltpu.VMEM((pairs, LANES, TAPS * LANES), bf16),
            pltpu.VMEM((pairs, ROWS, LANES), f32),
            pltpu.VMEM((sz.tiles, pairs, LANES), f32),
            pltpu.VMEM((sz.tiles, pairs, LANES), bf16),
            pltpu.VMEM((2, pairs, sz.ny, pad, LANES), bf16),
            pltpu.VMEM((pairs, sz.ny, pad, LANES), bf16),
            pltpu.VMEM((pairs, sz.ny, pad, LANES), bf16),
            pltpu.VMEM((sz.ny - 1, pairs, pad, LANES), bf16),
            pltpu.VMEM((pairs, pad, LANES), bf16),
            pltpu.VMEM((sz.nz // 4, sz.nx - 1, sz.ny, pad, LANES), bf16),
            pltpu.VMEM((sz.nz // 4, sz.ny, pad, LANES), bf16),
            pltpu.VMEM((sz.nz, sz.nx, pad, LANES), bf16),
            pltpu.VMEM((pad, LANES), f32),
            pltpu.VMEM((pad, LANES), bf16),
            pltpu.VMEM((sz.ny, pad, LANES), bf16),
            pltpu.VMEM((sz.nx - 1, sz.nz, pairs, LANES), bf16),
            pltpu.VMEM((sz.nz, pairs, LANES), bf16),
            pltpu.VMEM((sz.nz - 1, pairs, LANES), bf16),
        ]
        + [dma((pairs,))] * 2
        + [dma((sz.nz - 1,))] * 2
        + [dma((sz.nx - 1,))] * 2
        + [dma((sz.nz - 1,))] * 2
        + [dma((sz.nx - 1,))] * 2
        + [dma((pairs,))] * 2
        + [dma((sz.ny - 1, pairs))] * 2
        + [dma((pairs,)), dma((sz.nz, sz.nx))]
        + [dma((sz.nz // 4, sz.nx - 1))] * 2
        + [dma((sz.nz // 4, sz.ny))]
        + [dma((sz.ny - 1,))] * 2
        + [dma((sz.ny,))] * 2
        + [dma((sz.nx - 1,))] * 2
        + [dma((sz.nz - 1,))] * 2,
        compiler_params=pltpu.CompilerParams(
            collective_id=0, has_side_effects=True, vmem_limit_bytes=56 * 1024 * 1024
        ),
        name="fused",
    )(counts, weights, slide_of[:, :, 0], owner_map, cot, tiles, conv_weight)
    pooled, input_grad, weight_grad = pl.pallas_call(
        finish_kernel,
        out_shape=results,
        in_specs=[vmem] * 3,
        out_specs=(hbm,) * 3,
        scratch_shapes=[dma((3,))],
        name="finish",
    )(*[pltpu.with_memory_space_constraint(v, pltpu.MemorySpace.VMEM) for v in made])
    input_grad = input_grad.reshape(1, SLOTS, SIDE, SIDE, channels)
    return pooled.reshape(1, 1, channels), input_grad, weight_grad


def solution(mesh):
    sz = Sizes(mesh)
    return jax.shard_map(
        functools.partial(shards, sz),
        mesh=mesh,
        in_specs=(
            P("slide", "tile", None, None, None),
            P("slide", "tile"),
            P("slide", "tile"),
            P("slide", "tile", None),
            P("slide", None),
            P("slide", "tile", None),
            P(),
        ),
        out_specs=(
            P("slide", "tile", None),
            P("slide", "tile", None, None, None),
            P(None, None, "tile"),
        ),
        check_vma=False,
    )
```

```python
import functools

import jax
import jax.numpy as jnp
from jax import lax
from jax.experimental import pallas as pl
from jax.experimental.pallas import tpu as pltpu
from jax.sharding import PartitionSpec as P

MESH = pl.DeviceIdType.MESH
LOSS_SCALE = 512.0
SIDE = 7
SLOTS = 3
WIDTH = 64
LANES = 128
TAPS = 9
ROWS = SLOTS * 64
BASE = 16
PADDED = BASE + ROWS + 16
f32 = jnp.float32
bf16 = jnp.bfloat16


class Sizes:
    def __init__(self, mesh):
        self.tiles = mesh.shape["tile"]
        self.slides = mesh.shape["slide"]
        self.ny = self.slides // 2
        self.nx = self.ny
        self.nz = self.tiles // self.nx
        self.pairs = self.tiles // 2
        self.share = 32 // self.ny
        self.packed = TAPS * self.share


def position(sz):
    tile = lax.axis_index("tile")
    slide = lax.axis_index("slide")
    return tile, slide, tile // sz.nz, tile % sz.nz, slide // 2, slide % 2


def remote(src, dst, send, recv, device):
    return pltpu.make_async_remote_copy(
        src_ref=src, dst_ref=dst, send_sem=send, recv_sem=recv, device_id=device, device_id_type=MESH
    )


def signal(device):
    pl.semaphore_signal(pltpu.get_barrier_semaphore(), inc=1, device_id=device, device_id_type=MESH)


def slot_route(slot, counts, weights, slide_of, owner_map):
    coef = jnp.where(slot < counts[0, 0], weights[0, slot], 0.0)
    return coef, owner_map[0, slide_of[0, slot]]


C_LAG = 3
Y_LAG = 12
X_LAG = 3
X_COUNT = 0
X_MIDDLE = 12
BARRIER_STEP = 0
Z_STEP = 6
P_STEP = 17


def fused_kernel(
    sz, counts, weights, slide_of, owner_map, cot, tiles_hbm, weight_hbm,
    pooled, input_grad, result,
    tiles, weight, stage, all_cot, my_total, z_total, x_total, total, grad,
    xp, gp, xc, gc, w_rows, w_lanes, slopes, parts, parts16,
    terms, c_in, s1, y_in, s2, x_in, s3, o_in, own, final, fin, px_in, psum, pz_in,
    tile_sem, weight_sem, gzs, gzr, gxs, gxr, tzs, tzr, txs, txr,
    cs, cr, ys, yr, os, orr, xs, xr, os3, fs, fr, ms, mr, pxs, pxr, pzs, pzr,
):
    tile, slide, x, z, y, c = position(sz)
    nx, ny, nz, pairs = sz.nx, sz.ny, sz.nz, sz.pairs
    share, nk = sz.share, nz // 2
    early, middle = min(X_COUNT, pairs), min(X_MIDDLE, pairs)
    z_peers = [(x * nz + (z + off) % nz, slide) for off in range(1, nz)]
    x_peers = [(((x + off) % nx) * nz + z, slide) for off in range(1, nx)]
    mate = (tile, y * 2 + 1 - c)
    y_peers = [(tile, ((y + off) % ny) * 2 + c) for off in range(1, ny)]
    is_owner = (z % 2) == c

    def owner_k(s):
        return (z // 2 + 1 + s // nx) % nk

    def pair_at(s):
        return ((x + 1 + s % nx) % nx) * nk + owner_k(s)

    def lanes_of(s):
        return pl.ds(pl.multiple_of(pair_at(s) * LANES, LANES), LANES)

    def load(s):
        lanes = lanes_of(s)
        return (
            pltpu.make_async_copy(tiles_hbm.at[0, :, :, :, lanes], tiles.at[s], tile_sem.at[s]),
            pltpu.make_async_copy(weight_hbm.at[:, :, lanes], weight.at[s], weight_sem.at[s]),
        )

    partners = z_peers + x_peers + y_peers + [mate]
    for peer in partners:
        signal(peer)

    for j in range(pairs):
        stage[pl.ds(j, 1), :] = cot[0, :, pl.ds(j * LANES, LANES)].astype(f32)
    all_cot[tile] = stage[...].astype(bf16)
    lane = lax.broadcasted_iota(jnp.int32, (8, LANES), 1)
    routes = [slot_route(s, counts, weights, slide_of, owner_map) for s in range(SLOTS)]
    mine = jnp.zeros((8, LANES), f32)
    for coef, target in routes:
        mine = mine + jnp.where(lane == target, coef, 0.0)
    my_total[...] = mine

    @pl.loop(0, pairs)
    def _(s):
        for copy in load(s):
            copy.start()

    xp[...] = jnp.zeros_like(xp)
    gp[...] = jnp.zeros_like(gp)

    def total_z(i):
        return remote(my_total, z_total.at[i], tzs.at[i], tzr.at[i], z_peers[i])

    def rows_z(i, source):
        return remote(all_cot.at[source], all_cot.at[source], gzs.at[i], gzr.at[i], z_peers[i])

    def total_x(i):
        return remote(total, x_total.at[i], txs.at[i], txr.at[i], x_peers[i])

    def rows_x(i, source):
        block = all_cot.at[pl.ds(source * nz, nz)]
        return remote(block, block, gxs.at[i], gxr.at[i], x_peers[i])

    low64 = lax.broadcasted_iota(jnp.int32, (WIDTH, LANES), 1) < WIDTH
    row = lax.broadcasted_iota(jnp.int32, (64, LANES), 0)
    real = (row % 8 < SIDE) & (row < 8 * SIDE)
    owner_row = lax.broadcasted_iota(jnp.int32, (sz.tiles, LANES), 0)

    @pl.loop(0, pairs)
    def _(s):
        @pl.when(s == BARRIER_STEP)
        def _():
            pl.semaphore_wait(pltpu.get_barrier_semaphore(), len(partners))
            for i in range(nz - 1):
                total_z(i).start()
                rows_z(i, tile).start()

        @pl.when(s == min(Z_STEP, pairs - 1))
        def _():
            v = my_total[...]
            for i in range(nz - 1):
                total_z(i).wait_recv()
                rows_z(i, x * nz + (z + nz - 1 - i) % nz).wait_recv()
                v = v + z_total[i]
            total[...] = v
            for i in range(nx - 1):
                total_x(i).start()
                rows_x(i, x).start()

        for copy in load(s):
            copy.wait()
        for tap in range(TAPS):
            w = weight[s, tap]
            zero = jnp.zeros_like(w)
            first, second = jnp.where(low64, w, zero), jnp.where(low64, zero, w)
            w_rows[pl.ds(tap * LANES, WIDTH), :] = first
            w_rows[pl.ds(tap * LANES + WIDTH, WIDTH), :] = second
            w_lanes[s, pl.ds(0, WIDTH), pl.ds(tap * LANES, LANES)] = first
            w_lanes[s, pl.ds(WIDTH, WIDTH), pl.ds(tap * LANES, LANES)] = second
        for t in range(SLOTS):
            for h in range(SIDE):
                xp[pl.ds(BASE + 64 * t + 8 * h, SIDE), :] = tiles[s, t, h].astype(f32)
        for tap in range(TAPS):
            shift = 8 * (tap // 3 - 1) + tap % 3 - 1
            xc[s, :, pl.ds(tap * LANES, LANES)] = xp[pl.ds(BASE + shift, ROWS), :].astype(bf16)
        pre = jnp.dot(xc[s], w_rows[...], preferred_element_type=f32)
        sigma = 1.0 / (1.0 + jnp.exp(-pre))
        part = jnp.zeros((sz.tiles, LANES), f32)
        for t in range(SLOTS):
            v, q = pre[64 * t : 64 * t + 64], sigma[64 * t : 64 * t + 64]
            mean = jnp.sum(jnp.where(real, v * q, 0.0), axis=0, keepdims=True) / (SIDE * SIDE)
            embedding = mean.astype(bf16).astype(f32)
            coef, target = routes[t]
            part = part + jnp.where(owner_row == target, coef, 0.0) * embedding
            slope = q * (1.0 + v * (1.0 - q))
            slopes[s, pl.ds(64 * t, 64), :] = jnp.where(real, slope, 0.0)
        parts[:, pl.ds(pair_at(s), 1), :] = part.reshape(sz.tiles, 1, LANES)

    def parts_x(i):
        xo = (x + i + 1) % nx
        return remote(parts16.at[pl.ds(xo * nz, nz)], px_in.at[i], pxs.at[i], pxr.at[i], x_peers[i])

    def parts_z(i):
        return remote(psum.at[(z + i + 1) % nz], pz_in.at[i], pzs.at[i], pzr.at[i], z_peers[i])

    parts16[...] = parts[...].astype(bf16)
    for i in range(nx - 1):
        parts_x(i).start()
    v = total[...]
    for i in range(nx - 1):
        total_x(i).wait_recv()
        rows_x(i, (x + nx - 1 - i) % nx).wait_recv()
        v = v + x_total[i]
    denominator = jnp.maximum(v, 1.0)

    def pick(owner):
        found = jnp.sum(jnp.where(lane == owner, denominator, 0.0), axis=1, keepdims=True)
        return jnp.broadcast_to(found[0:1], (pairs, LANES))

    for t, (coef, target) in enumerate(routes):
        scaled = (LOSS_SCALE * all_cot[target].astype(f32) / pick(target)).astype(bf16)
        grad[t] = coef * scaled.astype(f32)

    def swap(s):
        return remote(terms.at[1 - c, s], c_in.at[s], cs.at[s], cr.at[s], mate)

    def along_y(i, s):
        return remote(s1.at[s, (y + i + 1) % ny], y_in.at[i, s], ys.at[i, s], yr.at[i, s], y_peers[i])

    def to_owner(s):
        device = (2 * pair_at(s) + c, slide)
        return remote(s2.at[s], o_in.at[z, x], os.at[s], orr.at[z, x], device)

    def along_x(s):
        device = (((x + 1 + s % nx) % nx) * nz + z, slide)
        m, i = s // (2 * nx), s % nx
        return remote(s1.at[s], x_in.at[m, i], xs.at[m, i], xr.at[m, i], device)

    def to_owner_y(s, q):
        device = (x * nz + 2 * owner_k(s) + c, q * 2 + c)
        m = s // (2 * nx)
        return remote(s3.at[m, q], o_in.at[z, y], os3.at[m, q], orr.at[z, y], device)

    def by_y(s):
        return (s // nx) % 2 == 0

    def mine_at(s, q):
        return is_owner & (owner_k(s) == z // 2) & (q == y)

    low = lax.broadcasted_iota(jnp.int32, (32, LANES), 1) < WIDTH

    def pre_grad(s):
        upstream = [grad[t, pl.ds(pair_at(s), 1), :] / (SIDE * SIDE) for t in range(SLOTS)]
        return [upstream[t] * slopes[s, pl.ds(64 * t, 64), :] for t in range(SLOTS)]

    def input_gradient(r):
        for t, rows in enumerate(pre_grad(r)):
            gp[pl.ds(BASE + 64 * t, 64), :] = rows
        for tap in range(TAPS):
            shift = 8 * (tap // 3 - 1) + tap % 3 - 1
            gc[:, pl.ds(tap * LANES, LANES)] = gp[pl.ds(BASE - shift, ROWS), :].astype(bf16)
        dx = lax.dot_general(
            gc[...], w_lanes[r], (((1,), (1,)), ((), ())), preferred_element_type=f32
        )
        lanes = lanes_of(r)
        for t in range(SLOTS):
            for h in range(SIDE):
                at = 64 * t + 8 * h
                input_grad[t, h, :, :, lanes] = dx[at : at + SIDE].reshape(SIDE, 1, LANES)

    @pl.loop(0, pairs + Y_LAG)
    def _(s):
        @pl.when(s < pairs)
        def _():
            g = jnp.concatenate(pre_grad(s), axis=0).astype(bf16)
            dw = jnp.dot(g.T, xc[s], preferred_element_type=f32)
            even, odd = [], []
            for tap in range(TAPS):
                d = dw[:, tap * LANES : (tap + 1) * LANES]
                even.append(jnp.where(low, d[0:32], pltpu.roll(d[32:64], WIDTH, 1)))
                odd.append(jnp.where(low, pltpu.roll(d[64:96], WIDTH, 1), d[96:128]))
            per = 16 // share
            for parity, rows in enumerate((even, odd)):
                for yy in range(ny):
                    for first in range(0, TAPS, per):
                        block = [v[yy * share : (yy + 1) * share] for v in rows[first : first + per]]
                        at = pl.ds(first * share, len(block) * share)
                        terms[parity, s, yy, at, :] = jnp.concatenate(block, axis=0).astype(bf16)
            swap(s).start()

        @pl.when((s >= X_LAG) & (s < early + X_LAG))
        def _():
            input_gradient(s - X_LAG)

        @pl.when((s >= C_LAG) & (s < pairs + C_LAG))
        def _():
            r = s - C_LAG
            swap(r).wait_recv()
            s1[r] = (terms[c, r].astype(f32) + c_in[r].astype(f32)).astype(bf16)

            @pl.when(by_y(r))
            def _():
                for i in range(ny - 1):
                    along_y(i, r).start()

            @pl.when(jnp.logical_not(by_y(r)) & (r % nx != nx - 1))
            def _():
                along_x(r).start()

        @pl.when((s >= Y_LAG) & by_y(s - Y_LAG))
        def _():
            r = s - Y_LAG
            v = s1[r, y].astype(f32)
            for i in range(ny - 1):
                along_y(i, r).wait_recv()
                v = v + y_in[i, r].astype(f32)
            s2[r] = v.astype(bf16)
            to_owner(r).start()

        @pl.when((s >= Y_LAG) & jnp.logical_not(by_y(s - Y_LAG)) & ((s - Y_LAG) % nx == nx - 1))
        def _():
            r = s - Y_LAG
            m = r // (2 * nx)
            v = s1[r].astype(f32)
            for i in range(nx - 1):
                along_x(r - nx + 1 + i).wait_recv()
                v = v + x_in[m, i].astype(f32)
            s3[m] = v.astype(bf16)
            for q in range(ny):

                @pl.when(jnp.logical_not(mine_at(r, q)))
                def _():
                    to_owner_y(r, q).start()

        @pl.when(s == min(P_STEP, pairs + Y_LAG - 1))
        def _():
            for i in range(nx - 1):
                parts_x(i).wait_recv()

            @pl.loop(0, nz)
            def _(k):
                v = parts[x * nz + k]
                for i in range(nx - 1):
                    v = v + px_in[i, k].astype(f32)
                psum[k] = v.astype(bf16)

            for i in range(nz - 1):
                parts_z(i).start()

    @pl.loop(early, middle)
    def _(s):
        input_gradient(s)

    v = psum[z].astype(f32)
    for i in range(nz - 1):
        parts_z(i).wait_recv()
        v = v + pz_in[i].astype(f32)
    pooled[...] = v / pick(tile)

    def final_y(i):
        return remote(final, fin.at[y], fs.at[i], fr.at[i], y_peers[i])

    def final_mate(i):
        piece = fin.at[(y + ny - i) % ny]
        return remote(piece, piece, ms.at[i], mr.at[i], mate)

    @pl.when(is_owner)
    def _():
        own[...] = s3[nk // 2 - 1, y].astype(f32)

        @pl.loop(0, sz.nz * nx)
        def _(d):
            from_z = 2 * ((z // 2 + nk - 1 - d // (2 * nx)) % nk) + (d // nx) % 2
            i = d % nx

            @pl.when(jnp.logical_not((from_z == z) & (i == y)))
            def _():
                remote(s2.at[0], o_in.at[from_z, i], os.at[0], orr.at[from_z, i], mate).wait_recv()
                own[...] += o_in[from_z, i].astype(f32)

        final[...] = (own[...] / LOSS_SCALE).astype(bf16)
        for i in range(ny - 1):
            final_y(i).start()
        fin[y] = final[...]
        final_mate(0).start()

    @pl.loop(middle, pairs)
    def _(s):
        input_gradient(s)

    for i in range(nz - 1):
        total_z(i).wait_send()
        rows_z(i, tile).wait_send()
        parts_z(i).wait_send()
    for i in range(nx - 1):
        total_x(i).wait_send()
        rows_x(i, x).wait_send()
        parts_x(i).wait_send()

    @pl.loop(0, pairs)
    def _(s):
        swap(s).wait_send()

        @pl.when(by_y(s))
        def _():
            for i in range(ny - 1):
                along_y(i, s).wait_send()
            to_owner(s).wait_send()

        @pl.when(jnp.logical_not(by_y(s)) & (s % nx != nx - 1))
        def _():
            along_x(s).wait_send()

        @pl.when(jnp.logical_not(by_y(s)) & (s % nx == nx - 1))
        def _():
            for q in range(ny):

                @pl.when(jnp.logical_not(mine_at(s, q)))
                def _():
                    to_owner_y(s, q).wait_send()

    @pl.when(is_owner)
    def _():
        for i in range(ny - 1):
            piece = fin.at[(y + ny - 1 - i) % ny]
            remote(final, piece, fs.at[i], fr.at[i], y_peers[i]).wait_recv()
            final_mate(i + 1).start()

    @pl.when(jnp.logical_not(is_owner))
    def _():
        for i in range(ny):
            final_mate(i).wait_recv()

    every = [fin[q].astype(f32) for q in range(ny)]
    for tap in range(TAPS):
        rows = [v[tap * share : (tap + 1) * share] for v in every]
        block = jnp.concatenate(rows, axis=0).T
        result[tap] = jnp.concatenate([block[0:WIDTH], block[WIDTH:]], axis=1)

    @pl.when(is_owner)
    def _():
        for i in range(ny - 1):
            final_y(i).wait_send()
        for i in range(ny):
            final_mate(i).wait_send()


def finish_kernel(a, b, c, a_out, b_out, c_out, sems):
    copies = [
        pltpu.make_async_copy(src, dst, sems.at[i])
        for i, (src, dst) in enumerate(((a, a_out), (b, b_out), (c, c_out)))
    ]
    for copy in copies:
        copy.start()
    for copy in copies:
        copy.wait()


def shards(sz, tiles, counts, weights, slide_of, owner_map, cot, conv_weight):
    pairs, channels = sz.pairs, sz.tiles * WIDTH
    smem = pl.BlockSpec(memory_space=pltpu.SMEM)
    vmem = pl.BlockSpec(memory_space=pltpu.VMEM)
    hbm = pl.BlockSpec(memory_space=pltpu.MemorySpace.HBM)
    dma = pltpu.SemaphoreType.DMA
    pad = sz.packed
    results = (
        jax.ShapeDtypeStruct((pairs, LANES), f32),
        jax.ShapeDtypeStruct((SLOTS, SIDE, SIDE, 1, channels), f32),
        jax.ShapeDtypeStruct((TAPS, WIDTH, WIDTH), f32),
    )
    made = pl.pallas_call(
        functools.partial(fused_kernel, sz),
        out_shape=tuple(pltpu.VMEM(r.shape, r.dtype) for r in results),
        in_specs=[smem] * 4 + [vmem] + [hbm] * 2,
        out_specs=(vmem, vmem, vmem),
        scratch_shapes=[
            pltpu.VMEM((pairs, SLOTS, SIDE, SIDE, LANES), bf16),
            pltpu.VMEM((pairs, TAPS, WIDTH, LANES), bf16),
            pltpu.VMEM((pairs, LANES), f32),
            pltpu.VMEM((sz.tiles, pairs, LANES), bf16),
            pltpu.VMEM((8, LANES), f32),
            pltpu.VMEM((sz.nz - 1, 8, LANES), f32),
            pltpu.VMEM((sz.nx - 1, 8, LANES), f32),
            pltpu.VMEM((8, LANES), f32),
            pltpu.VMEM((SLOTS, pairs, LANES), f32),
            pltpu.VMEM((PADDED, LANES), f32),
            pltpu.VMEM((PADDED, LANES), f32),
            pltpu.VMEM((pairs, ROWS, TAPS * LANES), bf16),
            pltpu.VMEM((ROWS, TAPS * LANES), bf16),
            pltpu.VMEM((TAPS * LANES, LANES), bf16),
            pltpu.VMEM((pairs, LANES, TAPS * LANES), bf16),
            pltpu.VMEM((pairs, ROWS, LANES), f32),
            pltpu.VMEM((sz.tiles, pairs, LANES), f32),
            pltpu.VMEM((sz.tiles, pairs, LANES), bf16),
            pltpu.VMEM((2, pairs, sz.ny, pad, LANES), bf16),
            pltpu.VMEM((pairs, sz.ny, pad, LANES), bf16),
            pltpu.VMEM((pairs, sz.ny, pad, LANES), bf16),
            pltpu.VMEM((sz.ny - 1, pairs, pad, LANES), bf16),
            pltpu.VMEM((pairs, pad, LANES), bf16),
            pltpu.VMEM((sz.nz // 4, sz.nx - 1, sz.ny, pad, LANES), bf16),
            pltpu.VMEM((sz.nz // 4, sz.ny, pad, LANES), bf16),
            pltpu.VMEM((sz.nz, sz.nx, pad, LANES), bf16),
            pltpu.VMEM((pad, LANES), f32),
            pltpu.VMEM((pad, LANES), bf16),
            pltpu.VMEM((sz.ny, pad, LANES), bf16),
            pltpu.VMEM((sz.nx - 1, sz.nz, pairs, LANES), bf16),
            pltpu.VMEM((sz.nz, pairs, LANES), bf16),
            pltpu.VMEM((sz.nz - 1, pairs, LANES), bf16),
        ]
        + [dma((pairs,))] * 2
        + [dma((sz.nz - 1,))] * 2
        + [dma((sz.nx - 1,))] * 2
        + [dma((sz.nz - 1,))] * 2
        + [dma((sz.nx - 1,))] * 2
        + [dma((pairs,))] * 2
        + [dma((sz.ny - 1, pairs))] * 2
        + [dma((pairs,)), dma((sz.nz, sz.nx))]
        + [dma((sz.nz // 4, sz.nx - 1))] * 2
        + [dma((sz.nz // 4, sz.ny))]
        + [dma((sz.ny - 1,))] * 2
        + [dma((sz.ny,))] * 2
        + [dma((sz.nx - 1,))] * 2
        + [dma((sz.nz - 1,))] * 2,
        compiler_params=pltpu.CompilerParams(
            collective_id=0, has_side_effects=True, vmem_limit_bytes=56 * 1024 * 1024
        ),
        name="fused",
    )(counts, weights, slide_of[:, :, 0], owner_map, cot, tiles, conv_weight)
    pooled, input_grad, weight_grad = pl.pallas_call(
        finish_kernel,
        out_shape=results,
        in_specs=[vmem] * 3,
        out_specs=(hbm,) * 3,
        scratch_shapes=[dma((3,))],
        name="finish",
    )(*[pltpu.with_memory_space_constraint(v, pltpu.MemorySpace.VMEM) for v in made])
    input_grad = input_grad.reshape(1, SLOTS, SIDE, SIDE, channels)
    return pooled.reshape(1, 1, channels), input_grad, weight_grad


def solution(mesh):
    sz = Sizes(mesh)
    return jax.shard_map(
        functools.partial(shards, sz),
        mesh=mesh,
        in_specs=(
            P("slide", "tile", None, None, None),
            P("slide", "tile"),
            P("slide", "tile"),
            P("slide", "tile", None),
            P("slide", None),
            P("slide", "tile", None),
            P(),
        ),
        out_specs=(
            P("slide", "tile", None),
            P("slide", "tile", None, None, None),
            P(None, None, "tile"),
        ),
        check_vma=False,
    )
```

```python
import functools

import jax
import jax.numpy as jnp
from jax import lax
from jax.experimental import pallas as pl
from jax.experimental.pallas import tpu as pltpu
from jax.sharding import PartitionSpec as P

MESH = pl.DeviceIdType.MESH
LOSS_SCALE = 512.0
SIDE = 7
SLOTS = 3
WIDTH = 64
LANES = 128
TAPS = 9
ROWS = SLOTS * 64
BASE = 16
PADDED = BASE + ROWS + 16
f32 = jnp.float32
bf16 = jnp.bfloat16


class Sizes:
    def __init__(self, mesh):
        self.tiles = mesh.shape["tile"]
        self.slides = mesh.shape["slide"]
        self.ny = self.slides // 2
        self.nx = self.ny
        self.nz = self.tiles // self.nx
        self.pairs = self.tiles // 2
        self.share = 32 // self.ny
        self.packed = TAPS * self.share


def position(sz):
    tile = lax.axis_index("tile")
    slide = lax.axis_index("slide")
    return tile, slide, tile // sz.nz, tile % sz.nz, slide // 2, slide % 2


def remote(src, dst, send, recv, device):
    return pltpu.make_async_remote_copy(
        src_ref=src, dst_ref=dst, send_sem=send, recv_sem=recv, device_id=device, device_id_type=MESH
    )


def signal(device):
    pl.semaphore_signal(pltpu.get_barrier_semaphore(), inc=1, device_id=device, device_id_type=MESH)


def slot_route(slot, counts, weights, slide_of, owner_map):
    coef = jnp.where(slot < counts[0, 0], weights[0, slot], 0.0)
    return coef, owner_map[0, slide_of[0, slot]]


C_LAG = 3
Y_LAG = 12
X_LAG = 3
X_COUNT = 0
X_MIDDLE = 12
BARRIER_STEP = 0
Z_STEP = 8
P_STEP = 20


def fused_kernel(
    sz, counts, weights, slide_of, owner_map, cot, tiles_hbm, weight_hbm,
    pooled, input_grad, result,
    tiles, weight, stage, all_cot, my_total, z_total, x_total, total, grad,
    xp, gp, xc, gc, w_rows, w_lanes, slopes, parts, parts16,
    terms, c_in, s1, y_in, s2, x_in, s3, o_in, own, final, fin, px_in, psum, pz_in,
    tile_sem, weight_sem, gzs, gzr, gxs, gxr, tzs, tzr, txs, txr,
    cs, cr, ys, yr, os, orr, xs, xr, os3, fs, fr, ms, mr, pxs, pxr, pzs, pzr,
):
    tile, slide, x, z, y, c = position(sz)
    nx, ny, nz, pairs = sz.nx, sz.ny, sz.nz, sz.pairs
    share, nk = sz.share, nz // 2
    early, middle = min(X_COUNT, pairs), min(X_MIDDLE, pairs)
    z_peers = [(x * nz + (z + off) % nz, slide) for off in range(1, nz)]
    x_peers = [(((x + off) % nx) * nz + z, slide) for off in range(1, nx)]
    mate = (tile, y * 2 + 1 - c)
    y_peers = [(tile, ((y + off) % ny) * 2 + c) for off in range(1, ny)]
    is_owner = (z % 2) == c

    def owner_k(s):
        return (z // 2 + 1 + s // nx) % nk

    def pair_at(s):
        return ((x + 1 + s % nx) % nx) * nk + owner_k(s)

    def lanes_of(s):
        return pl.ds(pl.multiple_of(pair_at(s) * LANES, LANES), LANES)

    def load(s):
        lanes = lanes_of(s)
        return (
            pltpu.make_async_copy(tiles_hbm.at[0, :, :, :, lanes], tiles.at[s], tile_sem.at[s]),
            pltpu.make_async_copy(weight_hbm.at[:, :, lanes], weight.at[s], weight_sem.at[s]),
        )

    partners = z_peers + x_peers + y_peers + [mate]
    for peer in partners:
        signal(peer)

    for j in range(pairs):
        stage[pl.ds(j, 1), :] = cot[0, :, pl.ds(j * LANES, LANES)].astype(f32)
    all_cot[tile] = stage[...].astype(bf16)
    lane = lax.broadcasted_iota(jnp.int32, (8, LANES), 1)
    routes = [slot_route(s, counts, weights, slide_of, owner_map) for s in range(SLOTS)]
    mine = jnp.zeros((8, LANES), f32)
    for coef, target in routes:
        mine = mine + jnp.where(lane == target, coef, 0.0)
    my_total[...] = mine

    @pl.loop(0, pairs)
    def _(s):
        for copy in load(s):
            copy.start()

    xp[...] = jnp.zeros_like(xp)
    gp[...] = jnp.zeros_like(gp)

    def total_z(i):
        return remote(my_total, z_total.at[i], tzs.at[i], tzr.at[i], z_peers[i])

    def rows_z(i, source):
        return remote(all_cot.at[source], all_cot.at[source], gzs.at[i], gzr.at[i], z_peers[i])

    def total_x(i):
        return remote(total, x_total.at[i], txs.at[i], txr.at[i], x_peers[i])

    def rows_x(i, source):
        block = all_cot.at[pl.ds(source * nz, nz)]
        return remote(block, block, gxs.at[i], gxr.at[i], x_peers[i])

    low64 = lax.broadcasted_iota(jnp.int32, (WIDTH, LANES), 1) < WIDTH
    row = lax.broadcasted_iota(jnp.int32, (64, LANES), 0)
    real = (row % 8 < SIDE) & (row < 8 * SIDE)
    owner_row = lax.broadcasted_iota(jnp.int32, (sz.tiles, LANES), 0)

    @pl.loop(0, pairs)
    def _(s):
        @pl.when(s == BARRIER_STEP)
        def _():
            pl.semaphore_wait(pltpu.get_barrier_semaphore(), len(partners))
            for i in range(nz - 1):
                total_z(i).start()
                rows_z(i, tile).start()

        @pl.when(s == min(Z_STEP, pairs - 1))
        def _():
            v = my_total[...]
            for i in range(nz - 1):
                total_z(i).wait_recv()
                rows_z(i, x * nz + (z + nz - 1 - i) % nz).wait_recv()
                v = v + z_total[i]
            total[...] = v
            for i in range(nx - 1):
                total_x(i).start()
                rows_x(i, x).start()

        for copy in load(s):
            copy.wait()
        for tap in range(TAPS):
            w = weight[s, tap]
            zero = jnp.zeros_like(w)
            first, second = jnp.where(low64, w, zero), jnp.where(low64, zero, w)
            w_rows[pl.ds(tap * LANES, WIDTH), :] = first
            w_rows[pl.ds(tap * LANES + WIDTH, WIDTH), :] = second
            w_lanes[s, pl.ds(0, WIDTH), pl.ds(tap * LANES, LANES)] = first
            w_lanes[s, pl.ds(WIDTH, WIDTH), pl.ds(tap * LANES, LANES)] = second
        for t in range(SLOTS):
            for h in range(SIDE):
                xp[pl.ds(BASE + 64 * t + 8 * h, SIDE), :] = tiles[s, t, h].astype(f32)
        for tap in range(TAPS):
            shift = 8 * (tap // 3 - 1) + tap % 3 - 1
            xc[s, :, pl.ds(tap * LANES, LANES)] = xp[pl.ds(BASE + shift, ROWS), :].astype(bf16)
        pre = jnp.dot(xc[s], w_rows[...], preferred_element_type=f32)
        sigma = 1.0 / (1.0 + jnp.exp(-pre))
        part = jnp.zeros((sz.tiles, LANES), f32)
        for t in range(SLOTS):
            v, q = pre[64 * t : 64 * t + 64], sigma[64 * t : 64 * t + 64]
            mean = jnp.sum(jnp.where(real, v * q, 0.0), axis=0, keepdims=True) / (SIDE * SIDE)
            embedding = mean.astype(bf16).astype(f32)
            coef, target = routes[t]
            part = part + jnp.where(owner_row == target, coef, 0.0) * embedding
            slope = q * (1.0 + v * (1.0 - q))
            slopes[s, pl.ds(64 * t, 64), :] = jnp.where(real, slope, 0.0)
        parts[:, pl.ds(pair_at(s), 1), :] = part.reshape(sz.tiles, 1, LANES)

    def parts_x(i):
        xo = (x + i + 1) % nx
        return remote(parts16.at[pl.ds(xo * nz, nz)], px_in.at[i], pxs.at[i], pxr.at[i], x_peers[i])

    def parts_z(i):
        return remote(psum.at[(z + i + 1) % nz], pz_in.at[i], pzs.at[i], pzr.at[i], z_peers[i])

    parts16[...] = parts[...].astype(bf16)
    for i in range(nx - 1):
        parts_x(i).start()
    v = total[...]
    for i in range(nx - 1):
        total_x(i).wait_recv()
        rows_x(i, (x + nx - 1 - i) % nx).wait_recv()
        v = v + x_total[i]
    denominator = jnp.maximum(v, 1.0)

    def pick(owner):
        found = jnp.sum(jnp.where(lane == owner, denominator, 0.0), axis=1, keepdims=True)
        return jnp.broadcast_to(found[0:1], (pairs, LANES))

    for t, (coef, target) in enumerate(routes):
        scaled = (LOSS_SCALE * all_cot[target].astype(f32) / pick(target)).astype(bf16)
        grad[t] = coef * scaled.astype(f32)

    def swap(s):
        return remote(terms.at[1 - c, s], c_in.at[s], cs.at[s], cr.at[s], mate)

    def along_y(i, s):
        return remote(s1.at[s, (y + i + 1) % ny], y_in.at[i, s], ys.at[i, s], yr.at[i, s], y_peers[i])

    def to_owner(s):
        device = (2 * pair_at(s) + c, slide)
        return remote(s2.at[s], o_in.at[z, x], os.at[s], orr.at[z, x], device)

    def along_x(s):
        device = (((x + 1 + s % nx) % nx) * nz + z, slide)
        m, i = s // (2 * nx), s % nx
        return remote(s1.at[s], x_in.at[m, i], xs.at[m, i], xr.at[m, i], device)

    def to_owner_y(s, q):
        device = (x * nz + 2 * owner_k(s) + c, q * 2 + c)
        m = s // (2 * nx)
        return remote(s3.at[m, q], o_in.at[z, y], os3.at[m, q], orr.at[z, y], device)

    def by_y(s):
        return (s // nx) % 2 == 0

    def mine_at(s, q):
        return is_owner & (owner_k(s) == z // 2) & (q == y)

    low = lax.broadcasted_iota(jnp.int32, (32, LANES), 1) < WIDTH

    def pre_grad(s):
        upstream = [grad[t, pl.ds(pair_at(s), 1), :] / (SIDE * SIDE) for t in range(SLOTS)]
        return [upstream[t] * slopes[s, pl.ds(64 * t, 64), :] for t in range(SLOTS)]

    def input_gradient(r):
        for t, rows in enumerate(pre_grad(r)):
            gp[pl.ds(BASE + 64 * t, 64), :] = rows
        for tap in range(TAPS):
            shift = 8 * (tap // 3 - 1) + tap % 3 - 1
            gc[:, pl.ds(tap * LANES, LANES)] = gp[pl.ds(BASE - shift, ROWS), :].astype(bf16)
        dx = lax.dot_general(
            gc[...], w_lanes[r], (((1,), (1,)), ((), ())), preferred_element_type=f32
        )
        lanes = lanes_of(r)
        for t in range(SLOTS):
            for h in range(SIDE):
                at = 64 * t + 8 * h
                input_grad[t, h, :, :, lanes] = dx[at : at + SIDE].reshape(SIDE, 1, LANES)

    @pl.loop(0, pairs + Y_LAG)
    def _(s):
        @pl.when(s < pairs)
        def _():
            g = jnp.concatenate(pre_grad(s), axis=0).astype(bf16)
            dw = jnp.dot(g.T, xc[s], preferred_element_type=f32)
            even, odd = [], []
            for tap in range(TAPS):
                d = dw[:, tap * LANES : (tap + 1) * LANES]
                even.append(jnp.where(low, d[0:32], pltpu.roll(d[32:64], WIDTH, 1)))
                odd.append(jnp.where(low, pltpu.roll(d[64:96], WIDTH, 1), d[96:128]))
            per = 16 // share
            for parity, rows in enumerate((even, odd)):
                for yy in range(ny):
                    for first in range(0, TAPS, per):
                        block = [v[yy * share : (yy + 1) * share] for v in rows[first : first + per]]
                        at = pl.ds(first * share, len(block) * share)
                        terms[parity, s, yy, at, :] = jnp.concatenate(block, axis=0).astype(bf16)
            swap(s).start()

        @pl.when((s >= X_LAG) & (s < early + X_LAG))
        def _():
            input_gradient(s - X_LAG)

        @pl.when((s >= C_LAG) & (s < pairs + C_LAG))
        def _():
            r = s - C_LAG
            swap(r).wait_recv()
            s1[r] = (terms[c, r].astype(f32) + c_in[r].astype(f32)).astype(bf16)

            @pl.when(by_y(r))
            def _():
                for i in range(ny - 1):
                    along_y(i, r).start()

            @pl.when(jnp.logical_not(by_y(r)) & (r % nx != nx - 1))
            def _():
                along_x(r).start()

        @pl.when((s >= Y_LAG) & by_y(s - Y_LAG))
        def _():
            r = s - Y_LAG
            v = s1[r, y].astype(f32)
            for i in range(ny - 1):
                along_y(i, r).wait_recv()
                v = v + y_in[i, r].astype(f32)
            s2[r] = v.astype(bf16)
            to_owner(r).start()

        @pl.when((s >= Y_LAG) & jnp.logical_not(by_y(s - Y_LAG)) & ((s - Y_LAG) % nx == nx - 1))
        def _():
            r = s - Y_LAG
            m = r // (2 * nx)
            v = s1[r].astype(f32)
            for i in range(nx - 1):
                along_x(r - nx + 1 + i).wait_recv()
                v = v + x_in[m, i].astype(f32)
            s3[m] = v.astype(bf16)
            for q in range(ny):

                @pl.when(jnp.logical_not(mine_at(r, q)))
                def _():
                    to_owner_y(r, q).start()

        @pl.when(s == min(P_STEP, pairs + Y_LAG - 1))
        def _():
            for i in range(nx - 1):
                parts_x(i).wait_recv()

            @pl.loop(0, nz)
            def _(k):
                v = parts[x * nz + k]
                for i in range(nx - 1):
                    v = v + px_in[i, k].astype(f32)
                psum[k] = v.astype(bf16)

            for i in range(nz - 1):
                parts_z(i).start()

    @pl.loop(early, middle)
    def _(s):
        input_gradient(s)

    v = psum[z].astype(f32)
    for i in range(nz - 1):
        parts_z(i).wait_recv()
        v = v + pz_in[i].astype(f32)
    pooled[...] = v / pick(tile)

    def final_y(i):
        return remote(final, fin.at[y], fs.at[i], fr.at[i], y_peers[i])

    def final_mate(i):
        piece = fin.at[(y + ny - i) % ny]
        return remote(piece, piece, ms.at[i], mr.at[i], mate)

    @pl.when(is_owner)
    def _():
        own[...] = s3[nk // 2 - 1, y].astype(f32)

        @pl.loop(0, sz.nz * nx)
        def _(d):
            from_z = 2 * ((z // 2 + nk - 1 - d // (2 * nx)) % nk) + (d // nx) % 2
            i = d % nx

            @pl.when(jnp.logical_not((from_z == z) & (i == y)))
            def _():
                remote(s2.at[0], o_in.at[from_z, i], os.at[0], orr.at[from_z, i], mate).wait_recv()
                own[...] += o_in[from_z, i].astype(f32)

        final[...] = (own[...] / LOSS_SCALE).astype(bf16)
        for i in range(ny - 1):
            final_y(i).start()
        fin[y] = final[...]
        final_mate(0).start()

    @pl.loop(middle, pairs)
    def _(s):
        input_gradient(s)

    for i in range(nz - 1):
        total_z(i).wait_send()
        rows_z(i, tile).wait_send()
        parts_z(i).wait_send()
    for i in range(nx - 1):
        total_x(i).wait_send()
        rows_x(i, x).wait_send()
        parts_x(i).wait_send()

    @pl.loop(0, pairs)
    def _(s):
        swap(s).wait_send()

        @pl.when(by_y(s))
        def _():
            for i in range(ny - 1):
                along_y(i, s).wait_send()
            to_owner(s).wait_send()

        @pl.when(jnp.logical_not(by_y(s)) & (s % nx != nx - 1))
        def _():
            along_x(s).wait_send()

        @pl.when(jnp.logical_not(by_y(s)) & (s % nx == nx - 1))
        def _():
            for q in range(ny):

                @pl.when(jnp.logical_not(mine_at(s, q)))
                def _():
                    to_owner_y(s, q).wait_send()

    @pl.when(is_owner)
    def _():
        for i in range(ny - 1):
            piece = fin.at[(y + ny - 1 - i) % ny]
            remote(final, piece, fs.at[i], fr.at[i], y_peers[i]).wait_recv()
            final_mate(i + 1).start()

    @pl.when(jnp.logical_not(is_owner))
    def _():
        for i in range(ny):
            final_mate(i).wait_recv()

    every = [fin[q].astype(f32) for q in range(ny)]
    for tap in range(TAPS):
        rows = [v[tap * share : (tap + 1) * share] for v in every]
        block = jnp.concatenate(rows, axis=0).T
        result[tap] = jnp.concatenate([block[0:WIDTH], block[WIDTH:]], axis=1)

    @pl.when(is_owner)
    def _():
        for i in range(ny - 1):
            final_y(i).wait_send()
        for i in range(ny):
            final_mate(i).wait_send()


def finish_kernel(a, b, c, a_out, b_out, c_out, sems):
    copies = [
        pltpu.make_async_copy(src, dst, sems.at[i])
        for i, (src, dst) in enumerate(((a, a_out), (b, b_out), (c, c_out)))
    ]
    for copy in copies:
        copy.start()
    for copy in copies:
        copy.wait()


def shards(sz, tiles, counts, weights, slide_of, owner_map, cot, conv_weight):
    pairs, channels = sz.pairs, sz.tiles * WIDTH
    smem = pl.BlockSpec(memory_space=pltpu.SMEM)
    vmem = pl.BlockSpec(memory_space=pltpu.VMEM)
    hbm = pl.BlockSpec(memory_space=pltpu.MemorySpace.HBM)
    dma = pltpu.SemaphoreType.DMA
    pad = sz.packed
    results = (
        jax.ShapeDtypeStruct((pairs, LANES), f32),
        jax.ShapeDtypeStruct((SLOTS, SIDE, SIDE, 1, channels), f32),
        jax.ShapeDtypeStruct((TAPS, WIDTH, WIDTH), f32),
    )
    made = pl.pallas_call(
        functools.partial(fused_kernel, sz),
        out_shape=tuple(pltpu.VMEM(r.shape, r.dtype) for r in results),
        in_specs=[smem] * 4 + [vmem] + [hbm] * 2,
        out_specs=(vmem, vmem, vmem),
        scratch_shapes=[
            pltpu.VMEM((pairs, SLOTS, SIDE, SIDE, LANES), bf16),
            pltpu.VMEM((pairs, TAPS, WIDTH, LANES), bf16),
            pltpu.VMEM((pairs, LANES), f32),
            pltpu.VMEM((sz.tiles, pairs, LANES), bf16),
            pltpu.VMEM((8, LANES), f32),
            pltpu.VMEM((sz.nz - 1, 8, LANES), f32),
            pltpu.VMEM((sz.nx - 1, 8, LANES), f32),
            pltpu.VMEM((8, LANES), f32),
            pltpu.VMEM((SLOTS, pairs, LANES), f32),
            pltpu.VMEM((PADDED, LANES), f32),
            pltpu.VMEM((PADDED, LANES), f32),
            pltpu.VMEM((pairs, ROWS, TAPS * LANES), bf16),
            pltpu.VMEM((ROWS, TAPS * LANES), bf16),
            pltpu.VMEM((TAPS * LANES, LANES), bf16),
            pltpu.VMEM((pairs, LANES, TAPS * LANES), bf16),
            pltpu.VMEM((pairs, ROWS, LANES), f32),
            pltpu.VMEM((sz.tiles, pairs, LANES), f32),
            pltpu.VMEM((sz.tiles, pairs, LANES), bf16),
            pltpu.VMEM((2, pairs, sz.ny, pad, LANES), bf16),
            pltpu.VMEM((pairs, sz.ny, pad, LANES), bf16),
            pltpu.VMEM((pairs, sz.ny, pad, LANES), bf16),
            pltpu.VMEM((sz.ny - 1, pairs, pad, LANES), bf16),
            pltpu.VMEM((pairs, pad, LANES), bf16),
            pltpu.VMEM((sz.nz // 4, sz.nx - 1, sz.ny, pad, LANES), bf16),
            pltpu.VMEM((sz.nz // 4, sz.ny, pad, LANES), bf16),
            pltpu.VMEM((sz.nz, sz.nx, pad, LANES), bf16),
            pltpu.VMEM((pad, LANES), f32),
            pltpu.VMEM((pad, LANES), bf16),
            pltpu.VMEM((sz.ny, pad, LANES), bf16),
            pltpu.VMEM((sz.nx - 1, sz.nz, pairs, LANES), bf16),
            pltpu.VMEM((sz.nz, pairs, LANES), bf16),
            pltpu.VMEM((sz.nz - 1, pairs, LANES), bf16),
        ]
        + [dma((pairs,))] * 2
        + [dma((sz.nz - 1,))] * 2
        + [dma((sz.nx - 1,))] * 2
        + [dma((sz.nz - 1,))] * 2
        + [dma((sz.nx - 1,))] * 2
        + [dma((pairs,))] * 2
        + [dma((sz.ny - 1, pairs))] * 2
        + [dma((pairs,)), dma((sz.nz, sz.nx))]
        + [dma((sz.nz // 4, sz.nx - 1))] * 2
        + [dma((sz.nz // 4, sz.ny))]
        + [dma((sz.ny - 1,))] * 2
        + [dma((sz.ny,))] * 2
        + [dma((sz.nx - 1,))] * 2
        + [dma((sz.nz - 1,))] * 2,
        compiler_params=pltpu.CompilerParams(
            collective_id=0, has_side_effects=True, vmem_limit_bytes=56 * 1024 * 1024
        ),
        name="fused",
    )(counts, weights, slide_of[:, :, 0], owner_map, cot, tiles, conv_weight)
    pooled, input_grad, weight_grad = pl.pallas_call(
        finish_kernel,
        out_shape=results,
        in_specs=[vmem] * 3,
        out_specs=(hbm,) * 3,
        scratch_shapes=[dma((3,))],
        name="finish",
    )(*[pltpu.with_memory_space_constraint(v, pltpu.MemorySpace.VMEM) for v in made])
    input_grad = input_grad.reshape(1, SLOTS, SIDE, SIDE, channels)
    return pooled.reshape(1, 1, channels), input_grad, weight_grad


def solution(mesh):
    sz = Sizes(mesh)
    return jax.shard_map(
        functools.partial(shards, sz),
        mesh=mesh,
        in_specs=(
            P("slide", "tile", None, None, None),
            P("slide", "tile"),
            P("slide", "tile"),
            P("slide", "tile", None),
            P("slide", None),
            P("slide", "tile", None),
            P(),
        ),
        out_specs=(
            P("slide", "tile", None),
            P("slide", "tile", None, None, None),
            P(None, None, "tile"),
        ),
        check_vma=False,
    )
```
